768 devices in a mesh: gx: 24 (over x, z_hi, core), gy: 32 (over y, z_lo).
Axes of the slice: x: 4, y: 8, z: 12 (z_hi: 3, z_lo: 4; z = z_hi * 4 + z_lo), core: 2. Of those that a mesh axis runs over, the one named last changes fastest.
Arguments:
- spectrum: bfloat16 [384, 512, 1152], P('gx', 'gy'), may hold values from 0.099609375 to 1
- courant: float32 [2, 1152], replicated, may hold values from -0.45 to 0.45
- source: float32 [384, 512], P('gx', 'gy'), may hold values from 0.2 to 2
- wave_land: int32 [384, 512], P('gx', 'gy'), may hold values 0 or 1
- stokes_kernel: bfloat16 [1152, 128], replicated, may hold values from -0.1875 to 0.1875
- velocity: float32 [768, 2048, 128], P('gx', 'gy'), may hold values from -6 to 6
- coriolis: float32 [768, 2048], P('gx', 'gy'), may hold values from 0.5 to 1.5
- ocean_codes: int32 [768, 2048, 4], P('gx', 'gy'), may hold values from 0 to 8
- ocean_weights: float32 [768, 2048, 4], P('gx', 'gy'), may hold values from 0.2 to 2
- wave_codes: int32 [384, 512, 4], P('gx', 'gy'), may hold values from 0 to 23
- wave_weights: float32 [384, 512, 4], P('gx', 'gy'), may hold values from 0.2 to 2
Outputs:
- new_spectrum: bfloat16 [384, 512, 1152], P('gx', 'gy')
- new_velocity: float32 [768, 2048, 128], P('gx', 'gy')
- wave_current: float32 [2, 384, 512], P(None, 'gx', 'gy')
The draws below stay inside these ranges and needn't reach their ends.
All inputs are finite; a program needn't handle non-finite values. No bound on the sum of `wave_land` on one device may be relied on, other than what follows from the above.
Results may differ from the reference program's by a relative error of at most 0.002.
Values may be sent and summed in bfloat16 or wider, within the bound.
A program may use at most 32 MiB of HBM per device.

```python
import math
import jax
import jax.numpy as jnp
from jax import lax

NB = 1152
NL = 64
K = 4
RX = 2
RY = 4
NWX = 384
NWY = 512
NOX = 768
NOY = 2048


def set_ends(drawn, stream_key, least, high):
    dims = drawn.shape
    place = [jax.random.randint(jax.random.fold_in(stream_key, axis), (), 0, dims[axis]) for axis in range(len(dims))]
    drawn = drawn.at[tuple(place)].set(least)
    longest = dims.index(max(dims))
    place[longest] = (place[longest] + 1) % dims[longest]
    return drawn.at[tuple(place)].set(high)


def steps_of(key, dims, shards, least, high):
    level = 1.0
    for position, parts in shards:
        draws = jax.random.uniform(jax.random.fold_in(jax.random.fold_in(key, 6), position), (parts,), jnp.float32, least / len(shards), high / len(shards))
        level = level * jnp.repeat(jnp.exp(draws), dims[position] // parts).reshape((-1,) + (1,) * (len(dims) - 1 - position))
    return level


def noise(stream_key, shape, width, bound, shards=(), held_as=jnp.bfloat16):
    level = steps_of(stream_key, shape, shards, -0.22, 0.18) if shards else 1.0
    result = jax.random.normal(stream_key, shape, jnp.float32) * width * level
    return jnp.minimum(jnp.maximum(result, -bound), bound).astype(held_as)


def setup_inputs(seed: int = 0) -> dict:
    seeds = jax.random.split(jax.random.key(seed), 12)
    spectrum = jnp.clip(jnp.exp(math.log(1.0) - 2.306499 * jax.random.uniform(seeds[0], (NWX, NWY, NB), jnp.float32) ** steps_of(seeds[0], (NWX, NWY, NB), ((0, 24), (1, 32)), -0.2, 0.2)), 0.099609375, 1.0).astype(jnp.bfloat16)
    courant = jnp.clip(jax.random.uniform(seeds[1], (2, NB), jnp.float32, -0.45, 0.45), -0.45, 0.45)
    source = jnp.clip(jnp.exp(math.log(2.0) - 2.3025851 * jax.random.uniform(seeds[2], (NWX, NWY), jnp.float32) ** steps_of(seeds[2], (NWX, NWY), ((0, 24), (1, 32)), -0.2, 0.2)), 0.2, 2.0)
    wave_land = set_ends((jax.random.randint(seeds[3], (NWX, NWY), 0, 4) < 3).astype(jnp.int32), jax.random.fold_in(seeds[3], 1), 0, 1)
    stokes_kernel = noise(seeds[4], (NB, 2 * NL), NB ** -0.5, 0.1875)
    velocity = noise(seeds[5], (NOX, NOY, 2 * NL), 1.0, 6.0, ((0, 24), (1, 32)), jnp.float32)
    coriolis = jnp.clip(0.5 + 1.0 * jax.random.uniform(seeds[6], (NOX, NOY), jnp.float32) ** steps_of(seeds[6], (NOX, NOY), ((0, 24), (1, 32)), -0.2, 0.2), 0.5, 1.5)
    ocean_codes = set_ends(jax.random.randint(seeds[7], (NOX, NOY, K), 0, 9), jax.random.fold_in(seeds[7], 1), 0, 8).astype(jnp.int32)
    ocean_weights = jnp.clip(jnp.exp(math.log(2.0) - 2.3025851 * jax.random.uniform(seeds[8], (NOX, NOY, K), jnp.float32) ** steps_of(seeds[8], (NOX, NOY, K), ((0, 24), (1, 32)), -0.2, 0.2)), 0.2, 2.0)
    wave_codes = set_ends(jax.random.randint(seeds[9], (NWX, NWY, K), 0, (RX + 2) * (RY + 2)), jax.random.fold_in(seeds[9], 1), 0, ((RX + 2) * (RY + 2)) - 1).astype(jnp.int32)
    wave_weights = jnp.clip(jnp.exp(math.log(2.0) - 2.3025851 * jax.random.uniform(seeds[10], (NWX, NWY, K), jnp.float32) ** steps_of(seeds[10], (NWX, NWY, K), ((0, 24), (1, 32)), -0.2, 0.2)), 0.2, 2.0)
    return {"spectrum": spectrum, "courant": courant, "source": source, "wave_land": wave_land, "stokes_kernel": stokes_kernel, "velocity": velocity, "coriolis": coriolis, "ocean_codes": ocean_codes, "ocean_weights": ocean_weights, "wave_codes": wave_codes, "wave_weights": wave_weights}


time_step = 0.5


def wave_rows(spectrum, courant, source, wave_land, stokes_kernel):
    speed_x = courant[0]
    speed_y = courant[1]

    def one_row(row_index):
        picked = jnp.take(spectrum, (row_index + jnp.arange(-1, 2, dtype=jnp.int32)) % NWX, axis=0).astype(jnp.float32)
        center = picked[1]
        padded = jnp.pad(center, ((1, 1), (0, 0)))
        advected = (center - jnp.maximum(speed_x, 0.0) * (center - picked[0])
                    - jnp.maximum(-speed_x, 0.0) * (center - picked[2])
                    - jnp.maximum(speed_y, 0.0) * (center - padded[:-2])
                    - jnp.maximum(-speed_y, 0.0) * (center - padded[2:]))
        land_row = jnp.take(wave_land, row_index, axis=0).astype(jnp.float32)[:, None]
        source_row = jnp.take(source, row_index, axis=0)[:, None]
        updated = (land_row * (advected + 0.2 * source_row * advected - 0.1 * advected * advected)).astype(jnp.bfloat16)
        profile = jnp.dot(updated, stokes_kernel, preferred_element_type=jnp.float32).astype(jnp.bfloat16)
        return updated, profile

    return lax.map(one_row, jnp.arange(NWX, dtype=jnp.int32))


def ocean_tendency(state, profiles_padded, coriolis, ocean_codes, ocean_weights):
    column = jnp.arange(NOY, dtype=jnp.int32)

    def one_row(row_index):
        rows = jnp.take(state, (row_index + jnp.arange(-2, 3, dtype=jnp.int32)) % NOX, axis=0)
        along_x = rows[:, :, NL:]
        dvdx = (8.0 * (along_x[3] - along_x[1]) - (along_x[4] - along_x[0])) / 12.0
        along_y = jnp.pad(rows[2, :, :NL], ((2, 2), (0, 0)))
        dudy = (8.0 * (along_y[3:-1] - along_y[1:-3]) - (along_y[4:] - along_y[:-4])) / 12.0
        codes = jnp.take(ocean_codes, row_index, axis=0)
        weights = jnp.take(ocean_weights, row_index, axis=0)
        normed = weights / jnp.sum(weights, axis=-1, keepdims=True)
        stokes = jnp.zeros((NOY, 2 * NL), jnp.float32)
        for entry in range(K):
            code = codes[:, entry]
            wave_x = (row_index // RX + code // 3 - 1) % NWX
            wave_y = column // RY + code % 3
            stokes = stokes + normed[:, entry:entry + 1] * profiles_padded[wave_x, wave_y].astype(jnp.float32)
        absolute = jnp.take(coriolis, row_index, axis=0)[:, None] + dvdx - dudy
        return jnp.concatenate([absolute * stokes[:, NL:], -absolute * stokes[:, :NL]], axis=-1)

    return lax.map(one_row, jnp.arange(NOX, dtype=jnp.int32))


def reference(spectrum, courant, source, wave_land, stokes_kernel, velocity, coriolis, ocean_codes, ocean_weights, wave_codes, wave_weights):
    new_spectrum, profiles = wave_rows(spectrum, courant, source, wave_land, stokes_kernel)
    profiles_padded = jnp.pad(profiles, ((0, 0), (1, 1), (0, 0)))
    first = ocean_tendency(velocity, profiles_padded, coriolis, ocean_codes, ocean_weights)
    middle = velocity + time_step * first
    second = ocean_tendency(middle, profiles_padded, coriolis, ocean_codes, ocean_weights)
    new_velocity = velocity + 0.5 * time_step * (first + second)
    means = jnp.stack([jnp.mean(new_velocity[:, :, :NL], axis=-1), jnp.mean(new_velocity[:, :, NL:], axis=-1)], axis=0)
    means_padded = jnp.pad(means, ((0, 0), (0, 0), (1, 1)))
    grid_x = lax.broadcasted_iota(jnp.int32, (NWX, NWY), 0)
    grid_y = lax.broadcasted_iota(jnp.int32, (NWX, NWY), 1)
    normed = wave_weights / jnp.sum(wave_weights, axis=-1, keepdims=True)
    current = jnp.zeros((2, NWX, NWY), jnp.float32)
    for entry in range(K):
        code = wave_codes[:, :, entry]
        ocean_x = (RX * grid_x + code // (RY + 2) - 1) % NOX
        ocean_y = RY * grid_y + code % (RY + 2)
        current = current + normed[None, :, :, entry] * means_padded[:, ocean_x, ocean_y]
    return new_spectrum, new_velocity, current
```

```python
import jax
import jax.numpy as jnp
from jax import lax
from jax.experimental import pallas as pl
from jax.experimental.pallas import tpu as pltpu
from jax.sharding import PartitionSpec as P

NL = 64
LEVELS = 2 * NL
K = 4
RX = 2
RY = 4
PITCH = 32
MESH = pl.DeviceIdType.MESH
F32 = jnp.float32
BF16 = jnp.bfloat16

time_step = 0.5


def kernel(
    size_x,
    size_y,
    spectrum_h,
    courant_h,
    source_h,
    land_h,
    stokes_h,
    velocity_h,
    coriolis_h,
    ocodes_h,
    oweights_h,
    wcodes_h,
    wweights_h,
    spectrum_o,
    velocity_o,
    current_o,
    cells,
    courant,
    source,
    land,
    stokes_kernel,
    wide,
    middle,
    coriolis,
    ocodes,
    oweights,
    wcodes,
    wweights,
    load_sem,
    edge_f,
    edge_s,
    edge_r,
    south_north,
    vx_s,
    vx_r,
    vy_s,
    vy_r,
    mx_s,
    mx_r,
    my_s,
    my_r,
    prof,
    px_s,
    px_r,
    py_s,
    py_r,
    pd_s,
    pd_r,
    select,
    stokes,
    cor,
    coef,
    means,
    ex_s,
    ex_r,
    ey_s,
    ey_r,
    ed_r,
    send_sem,
    recv_sem,
):
    wx, wy, bins = spectrum_o.shape
    ox, oy = velocity_o.shape[:2]
    ix, iy = lax.axis_index("gx"), lax.axis_index("gy")
    at_south, at_north = iy == 0, iy == size_y - 1

    def peer(dx, dy):
        return (lax.rem(ix + dx + size_x, size_x), lax.rem(iy + dy + size_y, size_y))

    straight = ((-1, 0), (1, 0), (0, -1), (0, 1))
    diagonal = ((-1, -1), (-1, 1), (1, -1), (1, 1))
    barrier = pltpu.get_barrier_semaphore()
    for step in straight + diagonal:
        pl.semaphore_signal(barrier, inc=1, device_id=peer(*step), device_id_type=MESH)

    loads = [
        pltpu.make_async_copy(src, dst, load_sem.at[i])
        for i, (src, dst) in enumerate(
            (
                (spectrum_h, cells.at[pl.ds(1, wx)]),
                (velocity_h, wide.at[pl.ds(2, ox), pl.ds(8, oy)]),
                (ocodes_h, ocodes),
                (oweights_h, oweights),
                (coriolis_h, coriolis),
                (wcodes_h, wcodes),
                (wweights_h, wweights),
                (courant_h, courant),
                (source_h, source),
                (land_h, land),
                (stokes_h, stokes_kernel),
            )
        )
    ]
    for load in loads:
        load.start()

    count = [0]

    def remote(src, dst, step):
        i = count[0]
        count[0] += 1
        return pltpu.make_async_remote_copy(
            src_ref=src,
            dst_ref=dst,
            send_sem=send_sem.at[i],
            recv_sem=recv_sem.at[i],
            device_id=peer(*step),
            device_id_type=MESH,
        )

    lane = lax.broadcasted_iota(jnp.int32, (1, LEVELS), 1)
    low = lane < NL

    def swap(value):
        return pltpu.roll(value, NL, 1)

    def pack_x(ref, side, row):
        edge = jnp.where(low, swap(ref[row, pl.ds(8, oy), :]), ref[row + 1, pl.ds(8, oy), :])
        side[...] = edge.astype(BF16)

    def pack_y(ref, side, col):
        edge = jnp.where(low, ref[pl.ds(2, ox), col, :], swap(ref[pl.ds(2, ox), col + 1, :]))
        side[...] = edge.astype(BF16)

    def unpack_x(ref, side, row):
        edge = side[...].astype(F32)
        ref[row, pl.ds(8, oy), :] = swap(edge)
        ref[row + 1, pl.ds(8, oy), :] = edge

    def unpack_y(ref, side, col, outside):
        edge = side[...].astype(F32)
        edge = jnp.where(outside, jnp.zeros_like(edge), edge)
        ref[pl.ds(2, ox), col, :] = edge
        ref[pl.ds(2, ox), col + 1, :] = swap(edge)

    loads[0].wait()
    for x in range(wx):
        row = cells[x + 1].astype(F32)
        edge_f[0, x : x + 1, :] = row[0:1]
        edge_f[1, x : x + 1, :] = row[wy - 1 : wy]
    edge_s[...] = edge_f[...].astype(BF16)
    loads[1].wait()
    pack_x(wide, vx_s.at[0], 2)
    pack_x(wide, vx_s.at[1], ox)
    pack_y(wide, vy_s.at[0], 8)
    pack_y(wide, vy_s.at[1], 6 + oy)

    pl.semaphore_wait(barrier, 8)
    first = [
        remote(cells.at[wx], cells.at[0], (1, 0)),
        remote(cells.at[1], cells.at[wx + 1], (-1, 0)),
        remote(edge_s.at[1], edge_r.at[0], (0, 1)),
        remote(edge_s.at[0], edge_r.at[1], (0, -1)),
        remote(vx_s.at[1], vx_r.at[0], (1, 0)),
        remote(vx_s.at[0], vx_r.at[1], (-1, 0)),
        remote(vy_s.at[1], vy_r.at[0], (0, 1)),
        remote(vy_s.at[0], vy_r.at[1], (0, -1)),
    ]
    for copy in first:
        copy.start()

    for load in loads[2:]:
        load.wait()
    prof[...] = jnp.zeros_like(prof)
    means[...] = jnp.zeros_like(means)
    speed_x, speed_y = courant[0:1, :], courant[1:2, :]
    coef[0:1, :] = 1.0 - jnp.abs(speed_x) - jnp.abs(speed_y)
    coef[1:2, :] = jnp.maximum(speed_x, 0.0)
    coef[2:3, :] = jnp.maximum(-speed_x, 0.0)
    coef[3:4, :] = jnp.maximum(speed_y, 0.0)
    coef[4:5, :] = jnp.maximum(-speed_y, 0.0)

    slot_row = lax.broadcasted_iota(jnp.int32, (LEVELS, LEVELS), 0)
    own_cell = lax.rem(lane, oy) // RY

    @pl.loop(0, wx)
    def _(i):
        def pair(ref, entry):
            return jnp.concatenate(
                [ref[RX * i, entry : entry + 1, :], ref[RX * i + 1, entry : entry + 1, :]], axis=1
            )

        weights = [pair(oweights, entry) for entry in range(K)]
        total = weights[0] + weights[1] + weights[2] + weights[3]
        rows = jnp.zeros((LEVELS, LEVELS), F32)
        for entry in range(K):
            code = pair(ocodes, entry)
            third = lax.shift_right_logical(code * 11, 5)
            slot = third * (PITCH - 3) + code + own_cell
            rows = rows + jnp.where(slot_row == slot, weights[entry] / total, 0.0)
        rows = rows.T
        high = rows.astype(BF16)
        select[i, :, 0:LEVELS] = high
        select[i, :, LEVELS : 2 * LEVELS] = (rows - high.astype(F32)).astype(BF16)

    turned = coriolis[...].T

    @pl.loop(0, ox)
    def _(x):
        here = lax.broadcasted_iota(jnp.int32, (oy, ox), 1) == x
        column = jnp.sum(jnp.where(here, turned, 0.0), axis=1, keepdims=True)
        cor[x] = jnp.broadcast_to(column, (oy, LEVELS))

    for copy in first[:4]:
        copy.wait()
    for side, outside in ((0, at_south), (1, at_north)):
        value = edge_r[side].astype(F32)
        south_north[side] = jnp.where(outside, jnp.zeros_like(value), value)

    growth = land[...].astype(F32)
    gain = (growth * (1.0 + 0.2 * source[...])).T
    damp = (0.1 * growth).T
    chunk = 3 * LEVELS
    cell_y = lax.broadcasted_iota(jnp.int32, (wy, chunk), 0)

    @pl.loop(0, wx)
    def _(x):
        here = lax.broadcasted_iota(jnp.int32, (wy, wx), 1) == x
        gain_x = jnp.sum(jnp.where(here, gain, 0.0), axis=1, keepdims=True)
        damp_x = jnp.sum(jnp.where(here, damp, 0.0), axis=1, keepdims=True)
        for start in range(0, bins, chunk):
            span = pl.ds(start, chunk)
            center = cells[x + 1, :, span].astype(F32)
            south = jnp.where(cell_y == 0, south_north[0, pl.ds(x, 1), span], pltpu.roll(center, 1, 0))
            north = jnp.where(
                cell_y == wy - 1, south_north[1, pl.ds(x, 1), span], pltpu.roll(center, wy - 1, 0)
            )
            advected = (
                coef[0:1, span] * center
                + coef[1:2, span] * cells[x, :, span].astype(F32)
                + coef[2:3, span] * cells[x + 2, :, span].astype(F32)
                + coef[3:4, span] * south
                + coef[4:5, span] * north
            )
            spectrum_o[x, :, span] = (advected * (gain_x - damp_x * advected)).astype(BF16)

    product = jnp.dot(
        spectrum_o[...].reshape(wx * wy, bins), stokes_kernel[...], preferred_element_type=F32
    )
    product = product.astype(BF16).astype(F32)
    product = jnp.where(low, swap(product), -swap(product)).reshape(wx, wy, LEVELS)
    prof[pl.ds(1, wx), pl.ds(1, wy), :] = product

    px_s[0] = product[0].astype(BF16)
    px_s[1] = product[wx - 1].astype(BF16)
    py_s[0] = prof[pl.ds(1, wx), 1, :].astype(BF16)
    py_s[1] = prof[pl.ds(1, wx), wy, :].astype(BF16)
    second = [
        remote(px_s.at[1], px_r.at[0], (1, 0)),
        remote(px_s.at[0], px_r.at[1], (-1, 0)),
        remote(py_s.at[1], py_r.at[0], (0, 1)),
        remote(py_s.at[0], py_r.at[1], (0, -1)),
        remote(px_s.at[1], pd_r.at[0], (1, 1)),
        remote(px_s.at[1], pd_r.at[1], (1, -1)),
        remote(px_s.at[0], pd_r.at[2], (-1, 1)),
        remote(px_s.at[0], pd_r.at[3], (-1, -1)),
    ]
    for copy in second:
        copy.start()
    for copy in first[4:]:
        copy.wait()
    unpack_x(wide, vx_r.at[0], 0)
    unpack_x(wide, vx_r.at[1], ox + 2)
    unpack_y(wide, vy_r.at[0], 6, at_south)
    unpack_y(wide, vy_r.at[1], 8 + oy, at_north)
    for copy in second:
        copy.wait()
    prof[0, pl.ds(1, wy), :] = px_r[0].astype(F32)
    prof[wx + 1, pl.ds(1, wy), :] = px_r[1].astype(F32)
    for side, outside, col in ((0, at_south, 0), (1, at_north, wy + 1)):
        value = py_r[side].astype(F32)
        prof[pl.ds(1, wx), col, :] = jnp.where(outside, jnp.zeros_like(value), value)
    for i, row, col, outside, line in (
        (0, 0, 0, at_south, wy - 1),
        (1, 0, wy + 1, at_north, 0),
        (2, wx + 1, 0, at_south, wy - 1),
        (3, wx + 1, wy + 1, at_north, 0),
    ):
        value = pd_r[i].astype(F32)[line : line + 1]
        prof[row, col : col + 1, :] = jnp.where(outside, jnp.zeros_like(value), value)

    c1 = jnp.where(low, -8.0 / 12.0, 8.0 / 12.0)
    c2 = jnp.where(low, -1.0 / 12.0, 1.0 / 12.0)

    def absolute(ref, x):
        near = jnp.where(low, ref[x + 2, pl.ds(9, oy), :], ref[x + 3, pl.ds(8, oy), :]) - jnp.where(
            low, ref[x + 2, pl.ds(7, oy), :], ref[x + 1, pl.ds(8, oy), :]
        )
        far = jnp.where(low, ref[x + 2, pl.ds(10, oy), :], ref[x + 4, pl.ds(8, oy), :]) - jnp.where(
            low, ref[x + 2, pl.ds(6, oy), :], ref[x, pl.ds(8, oy), :]
        )
        turn = c1 * near - c2 * far
        return cor[x] + turn + swap(turn)

    @pl.loop(0, wx)
    def _(i):
        block = prof[pl.ds(i, 4)].reshape(4 * PITCH, LEVELS).astype(BF16)
        block = jnp.concatenate([block, block], axis=0)
        both = jnp.dot(select[i], block, preferred_element_type=F32)
        for part in range(RX):
            x = RX * i + part
            drift = both[part * oy : (part + 1) * oy]
            stokes[x] = drift
            middle[x + 2, pl.ds(8, oy), :] = (
                wide[x + 2, pl.ds(8, oy), :] + time_step * absolute(wide, x) * drift
            )

    pack_x(middle, mx_s.at[0], 2)
    pack_x(middle, mx_s.at[1], ox)
    pack_y(middle, my_s.at[0], 8)
    pack_y(middle, my_s.at[1], 6 + oy)
    third = [
        remote(mx_s.at[1], mx_r.at[0], (1, 0)),
        remote(mx_s.at[0], mx_r.at[1], (-1, 0)),
        remote(my_s.at[1], my_r.at[0], (0, 1)),
        remote(my_s.at[0], my_r.at[1], (0, -1)),
    ]
    for copy in third:
        copy.start()
    for copy in third:
        copy.wait()
    unpack_x(middle, mx_r.at[0], 0)
    unpack_x(middle, mx_r.at[1], ox + 2)
    unpack_y(middle, my_r.at[0], 6, at_south)
    unpack_y(middle, my_r.at[1], 8 + oy, at_north)

    def finish(x, by_column):
        rate = absolute(middle, x) * stokes[x]
        value = (
            0.5 * (wide[x + 2, pl.ds(8, oy), :] + middle[x + 2, pl.ds(8, oy), :])
            + (0.5 * time_step) * rate
        )
        velocity_o[x] = value
        mean_u = jnp.sum(jnp.where(low, value, 0.0), axis=1, keepdims=True)
        mean_v = jnp.sum(jnp.where(low, 0.0, value), axis=1, keepdims=True)
        by_column = jnp.where(lane == x, mean_u, by_column)
        return jnp.where(lane == x + NL, mean_v, by_column)

    by_column = lax.fori_loop(0, ox, finish, jnp.zeros((oy, LEVELS), F32)) * (1.0 / NL)
    by_row = jnp.concatenate([by_column, jnp.zeros((LEVELS - oy, LEVELS), F32)], axis=0).T
    for c in range(2):
        rows = by_row[c * NL : c * NL + ox]
        means[c, pl.ds(8, ox), :] = rows
        ex_s[0, c : c + 1, :] = rows[0:1]
        ex_s[1, c : c + 1, :] = rows[ox - 1 : ox]
    ey_s[0] = by_column[0:8]
    ey_s[1] = by_column[oy - 8 : oy]
    fourth = [
        remote(ex_s.at[1], ex_r.at[0], (1, 0)),
        remote(ex_s.at[0], ex_r.at[1], (-1, 0)),
        remote(ey_s.at[1], ey_r.at[0], (0, 1)),
        remote(ey_s.at[0], ey_r.at[1], (0, -1)),
        remote(ey_s.at[1], ed_r.at[0], (1, 1)),
        remote(ey_s.at[0], ed_r.at[1], (1, -1)),
        remote(ey_s.at[1], ed_r.at[2], (-1, 1)),
        remote(ey_s.at[0], ed_r.at[3], (-1, -1)),
    ]
    for copy in fourth:
        copy.start()

    target = lax.broadcasted_iota(jnp.int32, (LEVELS, LEVELS), 1)
    origin = lax.broadcasted_iota(jnp.int32, (LEVELS, LEVELS), 0)
    offset = RY * lax.rem(target, wy) + target // wy - 1
    used = lane < (RY + 2) * wy
    spread = jnp.where((origin == (offset & (LEVELS - 1))) & used, 1.0, 0.0)
    repeat = LEVELS // wy
    wave_sum = wweights[:, 0, :] + wweights[:, 1, :] + wweights[:, 2, :] + wweights[:, 3, :]
    tiled = [
        (
            jnp.concatenate([wcodes[:, entry, :]] * repeat, axis=1),
            jnp.concatenate([wweights[:, entry, :] / wave_sum] * repeat, axis=1),
        )
        for entry in range(K)
    ]
    wanted = []
    for a in range(RX + 2):
        number = (RY + 2) * a + lane // wy
        chosen = jnp.zeros((wx, LEVELS), F32)
        for code, weight in tiled:
            chosen = chosen + jnp.where((code == number) & used, weight, 0.0)
        wanted.append(chosen)

    for copy in fourth:
        copy.wait()
    for c in range(2):
        means[c, 7:8, :] = ex_r[0, c : c + 1, :]
        means[c, 8 + ox : 9 + ox, :] = ex_r[1, c : c + 1, :]
    for side, line, outside, spot, near in (
        (0, 7, at_south, LEVELS - 1, (0, 2)),
        (1, 0, at_north, oy, (1, 3)),
    ):
        here = lane == spot
        column = ey_r[side].T[:, line : line + 1]
        for c in range(2):
            inner = column[c * NL : c * NL + ox]
            inner = jnp.where(outside, jnp.zeros_like(inner), inner)
            means[c, pl.ds(8, ox), :] = jnp.where(here, inner, means[c, pl.ds(8, ox), :])
            for index, row, source_x in ((near[0], 7, ox - 1), (near[1], 8 + ox, 0)):
                spot_x = c * NL + source_x
                corner = ed_r[index, line : line + 1, spot_x : spot_x + 1]
                corner = jnp.where(outside, jnp.zeros_like(corner), corner)
                means[c, row : row + 1, :] = jnp.where(here, corner, means[c, row : row + 1, :])

    gathered = jnp.concatenate(
        [means[c, pl.ds(7 + a, wx, stride=RX), :] for a in range(RX + 2) for c in range(2)], axis=0
    )
    gathered = jnp.dot(
        gathered, spread, preferred_element_type=F32, precision=lax.Precision.HIGHEST
    )
    for c in range(2):
        total = jnp.zeros((wx, LEVELS), F32)
        for a in range(RX + 2):
            start = (2 * a + c) * wx
            total = total + gathered[start : start + wx] * wanted[a]
        shift = LEVELS // 2
        while shift >= wy:
            total = total + pltpu.roll(total, shift, 1)
            shift //= 2
        current_o[c] = total[:, :wy]


def solution(mesh):
    size_x, size_y = mesh.shape["gx"], mesh.shape["gy"]

    def step(
        spectrum,
        courant,
        source,
        wave_land,
        stokes_kernel,
        velocity,
        coriolis,
        ocean_codes,
        ocean_weights,
        wave_codes,
        wave_weights,
    ):
        wx, wy, bins = spectrum.shape
        ox, oy, levels = velocity.shape
        turn = lambda value: jnp.transpose(value, (0, 2, 1))
        operands = (
            spectrum,
            courant,
            source,
            wave_land,
            stokes_kernel,
            velocity,
            coriolis,
            turn(ocean_codes),
            turn(ocean_weights),
            turn(wave_codes),
            turn(wave_weights),
        )
        vmem = pltpu.VMEM
        edge_x = vmem((2, oy, levels), BF16)
        edge_y = vmem((2, ox, levels), BF16)
        prof_edge = vmem((2, wx, levels), BF16)
        tile = vmem((2, 8, levels), F32)
        copies = 28
        scratch = [
            vmem((wx + 2, wy, bins), BF16),
            vmem((2, bins), F32),
            vmem((wx, wy), F32),
            vmem((wx, wy), jnp.int32),
            vmem((bins, levels), BF16),
            vmem((ox + 4, oy + 16, levels), F32),
            vmem((ox + 4, oy + 16, levels), F32),
            vmem((ox, oy), F32),
            vmem((ox, K, oy), jnp.int32),
            vmem((ox, K, oy), F32),
            vmem((wx, K, wy), jnp.int32),
            vmem((wx, K, wy), F32),
            pltpu.SemaphoreType.DMA((11,)),
            vmem((2, wx, bins), F32),
            vmem((2, wx, bins), BF16),
            vmem((2, wx, bins), BF16),
            vmem((2, wx, bins), F32),
            edge_x,
            edge_x,
            edge_y,
            edge_y,
            edge_x,
            edge_x,
            edge_y,
            edge_y,
            vmem((wx + 3, PITCH, levels), F32),
            prof_edge,
            prof_edge,
            prof_edge,
            prof_edge,
            prof_edge,
            vmem((4, wx, levels), BF16),
            vmem((wx, levels, 2 * levels), BF16),
            vmem((ox, oy, levels), F32),
            vmem((ox, oy, levels), F32),
            vmem((8, bins), F32),
            vmem((2, ox + 16, levels), F32),
            tile,
            tile,
            tile,
            tile,
            vmem((4, 8, levels), F32),
            pltpu.SemaphoreType.DMA((copies,)),
            pltpu.SemaphoreType.DMA((copies,)),
        ]
        body = lambda *refs: kernel(size_x, size_y, *refs)
        return pl.pallas_call(
            body,
            out_shape=(
                jax.ShapeDtypeStruct((wx, wy, bins), BF16),
                jax.ShapeDtypeStruct((ox, oy, levels), F32),
                jax.ShapeDtypeStruct((2, wx, wy), F32),
            ),
            in_specs=[pl.BlockSpec(memory_space=pltpu.HBM)] * len(operands),
            out_specs=(pl.BlockSpec(memory_space=pltpu.VMEM),) * 3,
            scratch_shapes=scratch,
            compiler_params=pltpu.CompilerParams(
                collective_id=0, has_side_effects=True, vmem_limit_bytes=65000000
            ),
            name="coupled_step",
        )(*operands)

    return jax.shard_map(
        step,
        mesh=mesh,
        in_specs=(
            P("gx", "gy", None),
            P(),
            P("gx", "gy"),
            P("gx", "gy"),
            P(),
            P("gx", "gy", None),
            P("gx", "gy"),
            P("gx", "gy", None),
            P("gx", "gy", None),
            P("gx", "gy", None),
            P("gx", "gy", None),
        ),
        out_specs=(P("gx", "gy", None), P("gx", "gy", None), P(None, "gx", "gy")),
        check_vma=False,
    )
```

```python
import jax
import jax.numpy as jnp
from jax import lax
from jax.experimental import pallas as pl
from jax.experimental.pallas import tpu as pltpu
from jax.sharding import PartitionSpec as P

NL = 64
LEVELS = 2 * NL
K = 4
RX = 2
RY = 4
PITCH = 32
MESH = pl.DeviceIdType.MESH
F32 = jnp.float32
BF16 = jnp.bfloat16

time_step = 0.5


def kernel(
    size_x,
    size_y,
    spectrum_h,
    courant_h,
    source_h,
    land_h,
    stokes_h,
    velocity_h,
    coriolis_h,
    ocodes_h,
    oweights_h,
    wcodes_h,
    wweights_h,
    spectrum_o,
    velocity_o,
    current_o,
    cells,
    courant,
    source,
    land,
    stokes_kernel,
    wide,
    middle,
    coriolis,
    ocodes,
    oweights,
    wcodes,
    wweights,
    load_sem,
    edge_f,
    edge_s,
    edge_r,
    south_north,
    vx_s,
    vx_r,
    vy_s,
    vy_r,
    mx_s,
    mx_r,
    my_s,
    my_r,
    strip,
    prof,
    px_s,
    px_r,
    py_s,
    py_r,
    pd_s,
    pd_r,
    select,
    stokes,
    cor,
    coef,
    means,
    ex_s,
    ex_r,
    ey_s,
    ey_r,
    ed_r,
    send_sem,
    recv_sem,
):
    wx, wy, bins = spectrum_o.shape
    ox, oy = velocity_o.shape[:2]
    ix, iy = lax.axis_index("gx"), lax.axis_index("gy")
    at_south, at_north = iy == 0, iy == size_y - 1

    def peer(dx, dy):
        return (lax.rem(ix + dx + size_x, size_x), lax.rem(iy + dy + size_y, size_y))

    straight = ((-1, 0), (1, 0), (0, -1), (0, 1))
    barrier = pltpu.get_barrier_semaphore()
    for step in straight:
        pl.semaphore_signal(barrier, inc=1, device_id=peer(*step), device_id_type=MESH)

    loads = [
        pltpu.make_async_copy(src, dst, load_sem.at[i])
        for i, (src, dst) in enumerate(
            (
                (spectrum_h, cells.at[pl.ds(1, wx)]),
                (velocity_h, wide.at[pl.ds(2, ox), pl.ds(8, oy)]),
                (ocodes_h, ocodes),
                (oweights_h, oweights),
                (coriolis_h, coriolis),
                (wcodes_h, wcodes),
                (wweights_h, wweights),
                (courant_h, courant),
                (source_h, source),
                (land_h, land),
                (stokes_h, stokes_kernel),
            )
        )
    ]
    for load in loads:
        load.start()

    count = [0]

    def remote(src, dst, step):
        i = count[0]
        count[0] += 1
        return pltpu.make_async_remote_copy(
            src_ref=src,
            dst_ref=dst,
            send_sem=send_sem.at[i],
            recv_sem=recv_sem.at[i],
            device_id=peer(*step),
            device_id_type=MESH,
        )

    lane = lax.broadcasted_iota(jnp.int32, (1, LEVELS), 1)
    low = lane < NL

    def swap(value):
        return pltpu.roll(value, NL, 1)

    def pack_x(ref, side, row):
        edge = jnp.where(low, swap(ref[row, pl.ds(8, oy), :]), ref[row + 1, pl.ds(8, oy), :])
        side[...] = edge.astype(BF16)

    def pack_y(ref, side, col):
        edge = jnp.where(low, ref[pl.ds(2, ox), col, :], swap(ref[pl.ds(2, ox), col + 1, :]))
        side[...] = edge.astype(BF16)

    def unpack_x(ref, side, row):
        edge = side[...].astype(F32)
        ref[row, pl.ds(8, oy), :] = swap(edge)
        ref[row + 1, pl.ds(8, oy), :] = edge

    def unpack_y(ref, side, col, outside):
        edge = side[...].astype(F32)
        edge = jnp.where(outside, jnp.zeros_like(edge), edge)
        ref[pl.ds(2, ox), col, :] = edge
        ref[pl.ds(2, ox), col + 1, :] = swap(edge)

    loads[0].wait()
    for x in range(wx):
        row = cells[x + 1].astype(F32)
        for slot, col in enumerate((0, 1, wy - 2, wy - 1)):
            edge_f[slot, x : x + 1, :] = row[col : col + 1]
    edge_s[0] = edge_f[0].astype(BF16)
    edge_s[1] = edge_f[3].astype(BF16)
    loads[1].wait()
    pack_x(wide, vx_s.at[0], 2)
    pack_x(wide, vx_s.at[1], ox)
    pack_y(wide, vy_s.at[0], 8)
    pack_y(wide, vy_s.at[1], 6 + oy)

    pl.semaphore_wait(barrier, 4)
    first = [
        remote(cells.at[wx], cells.at[0], (1, 0)),
        remote(cells.at[1], cells.at[wx + 1], (-1, 0)),
        remote(edge_s.at[1], edge_r.at[0], (0, 1)),
        remote(edge_s.at[0], edge_r.at[1], (0, -1)),
        remote(vx_s.at[1], vx_r.at[0], (1, 0)),
        remote(vx_s.at[0], vx_r.at[1], (-1, 0)),
        remote(vy_s.at[1], vy_r.at[0], (0, 1)),
        remote(vy_s.at[0], vy_r.at[1], (0, -1)),
    ]
    for copy in first:
        copy.start()

    for load in loads[2:]:
        load.wait()
    prof[...] = jnp.zeros_like(prof)
    means[...] = jnp.zeros_like(means)
    speed_x, speed_y = courant[0:1, :], courant[1:2, :]
    coef[0:1, :] = 1.0 - jnp.abs(speed_x) - jnp.abs(speed_y)
    coef[1:2, :] = jnp.maximum(speed_x, 0.0)
    coef[2:3, :] = jnp.maximum(-speed_x, 0.0)
    coef[3:4, :] = jnp.maximum(speed_y, 0.0)
    coef[4:5, :] = jnp.maximum(-speed_y, 0.0)

    slot_row = lax.broadcasted_iota(jnp.int32, (LEVELS, LEVELS), 0)
    own_cell = lax.rem(lane, oy) // RY

    @pl.loop(0, wx)
    def _(i):
        def pair(ref, entry):
            return jnp.concatenate(
                [ref[RX * i, entry : entry + 1, :], ref[RX * i + 1, entry : entry + 1, :]], axis=1
            )

        weights = [pair(oweights, entry) for entry in range(K)]
        total = weights[0] + weights[1] + weights[2] + weights[3]
        rows = jnp.zeros((LEVELS, LEVELS), F32)
        for entry in range(K):
            code = pair(ocodes, entry)
            third = lax.shift_right_logical(code * 11, 5)
            slot = third * (PITCH - 3) + code + own_cell
            rows = rows + jnp.where(slot_row == slot, weights[entry] / total, 0.0)
        rows = rows.T
        high = rows.astype(BF16)
        select[i, :, 0:LEVELS] = high
        select[i, :, LEVELS : 2 * LEVELS] = (rows - high.astype(F32)).astype(BF16)

    turned = coriolis[...].T

    @pl.loop(0, ox)
    def _(x):
        here = lax.broadcasted_iota(jnp.int32, (oy, ox), 1) == x
        column = jnp.sum(jnp.where(here, turned, 0.0), axis=1, keepdims=True)
        cor[x] = jnp.broadcast_to(column, (oy, LEVELS))

    for copy in first[:4]:
        copy.wait()
    for side, outside in ((0, at_south), (1, at_north)):
        value = edge_r[side].astype(F32)
        south_north[side] = jnp.where(outside, jnp.zeros_like(value), value)

    growth = land[...].astype(F32)
    gain_rows = growth * (1.0 + 0.2 * source[...])
    damp_rows = 0.1 * growth
    gain, damp = gain_rows.T, damp_rows.T
    chunk = 3 * LEVELS
    cell_x = lax.broadcasted_iota(jnp.int32, (wx, chunk), 0)
    cell_y = lax.broadcasted_iota(jnp.int32, (wy, chunk), 0)

    def updated(span, center, west, east, south, north, gain_x, damp_x):
        advected = (
            coef[0:1, span] * center
            + coef[1:2, span] * west
            + coef[2:3, span] * east
            + coef[3:4, span] * south
            + coef[4:5, span] * north
        )
        return (advected * (gain_x - damp_x * advected)).astype(BF16)

    def update_row(x):
        here = lax.broadcasted_iota(jnp.int32, (wy, wx), 1) == x
        gain_x = jnp.sum(jnp.where(here, gain, 0.0), axis=1, keepdims=True)
        damp_x = jnp.sum(jnp.where(here, damp, 0.0), axis=1, keepdims=True)
        for start in range(0, bins, chunk):
            span = pl.ds(start, chunk)
            center = cells[x + 1, :, span].astype(F32)
            south = jnp.where(cell_y == 0, south_north[0, pl.ds(x, 1), span], pltpu.roll(center, 1, 0))
            north = jnp.where(
                cell_y == wy - 1, south_north[1, pl.ds(x, 1), span], pltpu.roll(center, wy - 1, 0)
            )
            west, east = cells[x, :, span].astype(F32), cells[x + 2, :, span].astype(F32)
            spectrum_o[x, :, span] = updated(span, center, west, east, south, north, gain_x, damp_x)

    def as_profile(value):
        value = jnp.dot(value, stokes_kernel[...], preferred_element_type=F32)
        value = value.astype(BF16).astype(F32)
        return jnp.where(low, swap(value), -swap(value))

    update_row(0)
    update_row(wx - 1)
    strip[0:wx] = spectrum_o[0]
    strip[wx : 2 * wx] = spectrum_o[wx - 1]
    for side, col in ((0, 0), (1, wy - 1)):
        for start in range(0, bins, chunk):
            span = pl.ds(start, chunk)
            center = edge_f[3 * side, :, span]
            before = cells[0, :, span].astype(F32)[col : col + 1]
            after = cells[wx + 1, :, span].astype(F32)[col : col + 1]
            west = jnp.where(cell_x == 0, before, pltpu.roll(center, 1, 0))
            east = jnp.where(cell_x == wx - 1, after, pltpu.roll(center, wx - 1, 0))
            inner, outer = edge_f[1 + side, :, span], south_north[side, :, span]
            south, north = (inner, outer) if side else (outer, inner)
            strip[(2 + side) * wx : (3 + side) * wx, span] = updated(
                span, center, west, east, south, north,
                gain_rows[:, col : col + 1], damp_rows[:, col : col + 1],
            )
    outermost = as_profile(strip[...]).astype(BF16)
    px_s[0] = outermost[0:wx]
    px_s[1] = outermost[wx : 2 * wx]
    py_s[0] = outermost[2 * wx : 3 * wx]
    py_s[1] = outermost[3 * wx : 4 * wx]
    second = [
        remote(px_s.at[1], px_r.at[0], (1, 0)),
        remote(px_s.at[0], px_r.at[1], (-1, 0)),
        remote(py_s.at[1], py_r.at[0], (0, 1)),
        remote(py_s.at[0], py_r.at[1], (0, -1)),
        remote(px_s.at[1], pd_r.at[0], (1, 1)),
        remote(px_s.at[1], pd_r.at[1], (1, -1)),
        remote(px_s.at[0], pd_r.at[2], (-1, 1)),
        remote(px_s.at[0], pd_r.at[3], (-1, -1)),
    ]
    for copy in second:
        copy.start()

    @pl.loop(1, wx - 1)
    def _(x):
        update_row(x)

    own = as_profile(spectrum_o[...].reshape(wx * wy, bins))
    prof[pl.ds(1, wx), pl.ds(1, wy), :] = own.reshape(wx, wy, LEVELS)
    for copy in first[4:]:
        copy.wait()
    unpack_x(wide, vx_r.at[0], 0)
    unpack_x(wide, vx_r.at[1], ox + 2)
    unpack_y(wide, vy_r.at[0], 6, at_south)
    unpack_y(wide, vy_r.at[1], 8 + oy, at_north)
    for copy in second:
        copy.wait()
    prof[0, pl.ds(1, wy), :] = px_r[0].astype(F32)
    prof[wx + 1, pl.ds(1, wy), :] = px_r[1].astype(F32)
    for side, outside, col in ((0, at_south, 0), (1, at_north, wy + 1)):
        value = py_r[side].astype(F32)
        prof[pl.ds(1, wx), col, :] = jnp.where(outside, jnp.zeros_like(value), value)
    for i, row, col, outside, line in (
        (0, 0, 0, at_south, wy - 1),
        (1, 0, wy + 1, at_north, 0),
        (2, wx + 1, 0, at_south, wy - 1),
        (3, wx + 1, wy + 1, at_north, 0),
    ):
        value = pd_r[i].astype(F32)[line : line + 1]
        prof[row, col : col + 1, :] = jnp.where(outside, jnp.zeros_like(value), value)

    c1 = jnp.where(low, -8.0 / 12.0, 8.0 / 12.0)
    c2 = jnp.where(low, -1.0 / 12.0, 1.0 / 12.0)

    def block(ref, x, rows, y, cols):
        return ref[pl.ds(x + 2, rows), pl.ds(y + 8, cols), :]

    def absolute(ref, x, rows, y, cols):
        def ahead(step):
            return jnp.where(
                low, block(ref, x, rows, y + step, cols), block(ref, x + step, rows, y, cols)
            )

        turn = c1 * (ahead(1) - ahead(-1)) - c2 * (ahead(2) - ahead(-2))
        return cor[pl.ds(x, rows), pl.ds(y, cols), :] + turn + pltpu.roll(turn, NL, 2)

    def advance(x, rows, y, cols):
        drift = stokes[pl.ds(x, rows), pl.ds(y, cols), :]
        middle[pl.ds(x + 2, rows), pl.ds(y + 8, cols), :] = (
            block(wide, x, rows, y, cols) + time_step * absolute(wide, x, rows, y, cols) * drift
        )

    @pl.loop(0, wx // 2)
    def _(pair):
        for part in range(2):
            i = 2 * pair + part
            near = prof[pl.ds(i, 4)].reshape(4 * PITCH, LEVELS).astype(BF16)
            near = jnp.concatenate([near, near], axis=0)
            both = jnp.dot(select[i], near, preferred_element_type=F32)
            stokes[pl.ds(RX * i, RX)] = both.reshape(RX, oy, LEVELS)

    advance(0, 2, 0, oy)
    advance(ox - 2, 2, 0, oy)

    @pl.loop(0, ox // 8)
    def _(i):
        advance(8 * i, 8, 0, 8)
        advance(8 * i, 8, oy - 8, 8)

    pack_x(middle, mx_s.at[0], 2)
    pack_x(middle, mx_s.at[1], ox)
    pack_y(middle, my_s.at[0], 8)
    pack_y(middle, my_s.at[1], 6 + oy)
    third = [
        remote(mx_s.at[1], mx_r.at[0], (1, 0)),
        remote(mx_s.at[0], mx_r.at[1], (-1, 0)),
        remote(my_s.at[1], my_r.at[0], (0, 1)),
        remote(my_s.at[0], my_r.at[1], (0, -1)),
    ]
    for copy in third:
        copy.start()

    @pl.loop(0, wx)
    def _(i):
        advance(RX * i, RX, 8, oy - 16)

    target = lax.broadcasted_iota(jnp.int32, (LEVELS, LEVELS), 1)
    origin = lax.broadcasted_iota(jnp.int32, (LEVELS, LEVELS), 0)
    offset = RY * lax.rem(target, wy) + target // wy - 1
    used = lane < (RY + 2) * wy
    spread = jnp.where((origin == (offset & (LEVELS - 1))) & used, 1.0, 0.0)
    repeat = LEVELS // wy
    wave_sum = wweights[:, 0, :] + wweights[:, 1, :] + wweights[:, 2, :] + wweights[:, 3, :]
    tiled = [
        (
            jnp.concatenate([wcodes[:, entry, :]] * repeat, axis=1),
            jnp.concatenate([wweights[:, entry, :] / wave_sum] * repeat, axis=1),
        )
        for entry in range(K)
    ]
    wanted = []
    for a in range(RX + 2):
        number = (RY + 2) * a + lane // wy
        chosen = jnp.zeros((wx, LEVELS), F32)
        for code, weight in tiled:
            chosen = chosen + jnp.where((code == number) & used, weight, 0.0)
        wanted.append(chosen)

    for copy in third:
        copy.wait()
    unpack_x(middle, mx_r.at[0], 0)
    unpack_x(middle, mx_r.at[1], ox + 2)
    unpack_y(middle, my_r.at[0], 6, at_south)
    unpack_y(middle, my_r.at[1], 8 + oy, at_north)

    def finish(x, rows, y, cols):
        rate = absolute(middle, x, rows, y, cols) * stokes[pl.ds(x, rows), pl.ds(y, cols), :]
        old = block(wide, x, rows, y, cols) + block(middle, x, rows, y, cols)
        value = 0.5 * old + (0.5 * time_step) * rate
        velocity_o[pl.ds(x, rows), pl.ds(y, cols), :] = value
        mean_u = jnp.sum(jnp.where(low, value, 0.0), axis=2, keepdims=True)
        mean_v = jnp.sum(jnp.where(low, 0.0, value), axis=2, keepdims=True)
        return mean_u * (1.0 / NL), mean_v * (1.0 / NL)

    def finish_into(table, x, rows, y, cols):
        mean_u, mean_v = finish(x, rows, y, cols)
        for row in range(rows):
            table = jnp.where(lane == x + row, mean_u[row], table)
            table = jnp.where(lane == x + row + NL, mean_v[row], table)
        return table

    ends = jnp.zeros((oy, LEVELS), F32)
    for side, x in ((0, 0), (1, ox - 1)):
        mean_u, mean_v = finish(x, 1, 0, oy)
        ends = jnp.where(lane == 2 * side, mean_u[0], ends)
        ends = jnp.where(lane == 2 * side + 1, mean_v[0], ends)
    ends = jnp.concatenate([ends, jnp.zeros((LEVELS - oy, LEVELS), F32)], axis=0).T
    ex_s[0, 0:2, :] = ends[0:2]
    ex_s[1, 0:2, :] = ends[2:4]

    def outer_columns(i, tables):
        return (
            finish_into(tables[0], 8 * i, 8, 0, 8),
            finish_into(tables[1], 8 * i, 8, oy - 8, 8),
        )

    nothing = jnp.zeros((8, LEVELS), F32)
    first_cols, last_cols = lax.fori_loop(0, ox // 8, outer_columns, (nothing, nothing))
    ey_s[0] = first_cols
    ey_s[1] = last_cols
    fourth = [
        remote(ex_s.at[1], ex_r.at[0], (1, 0)),
        remote(ex_s.at[0], ex_r.at[1], (-1, 0)),
        remote(ey_s.at[1], ey_r.at[0], (0, 1)),
        remote(ey_s.at[0], ey_r.at[1], (0, -1)),
        remote(ey_s.at[1], ed_r.at[0], (1, 1)),
        remote(ey_s.at[0], ed_r.at[1], (1, -1)),
        remote(ey_s.at[1], ed_r.at[2], (-1, 1)),
        remote(ey_s.at[0], ed_r.at[3], (-1, -1)),
    ]
    for copy in fourth:
        copy.start()

    inner_cols = lax.fori_loop(
        0,
        wx,
        lambda i, table: finish_into(table, RX * i, RX, 8, oy - 16),
        jnp.zeros((oy - 16, LEVELS), F32),
    )
    blank = jnp.zeros((LEVELS - oy, LEVELS), F32)
    by_row = jnp.concatenate([first_cols, inner_cols, last_cols, blank], axis=0).T
    for c in range(2):
        means[c, pl.ds(8, ox), :] = by_row[c * NL : c * NL + ox]

    for copy in fourth:
        copy.wait()
    for c in range(2):
        means[c, 7:8, :] = ex_r[0, c : c + 1, :]
        means[c, 8 + ox : 9 + ox, :] = ex_r[1, c : c + 1, :]
    for side, line, outside, spot, near in (
        (0, 7, at_south, LEVELS - 1, (0, 2)),
        (1, 0, at_north, oy, (1, 3)),
    ):
        here = lane == spot
        column = ey_r[side].T[:, line : line + 1]
        for c in range(2):
            inner = column[c * NL : c * NL + ox]
            inner = jnp.where(outside, jnp.zeros_like(inner), inner)
            means[c, pl.ds(8, ox), :] = jnp.where(here, inner, means[c, pl.ds(8, ox), :])
            for index, row, source_x in ((near[0], 7, ox - 1), (near[1], 8 + ox, 0)):
                spot_x = c * NL + source_x
                corner = ed_r[index, line : line + 1, spot_x : spot_x + 1]
                corner = jnp.where(outside, jnp.zeros_like(corner), corner)
                means[c, row : row + 1, :] = jnp.where(here, corner, means[c, row : row + 1, :])

    gathered = jnp.concatenate(
        [means[c, pl.ds(7 + a, wx, stride=RX), :] for a in range(RX + 2) for c in range(2)], axis=0
    )
    gathered = jnp.dot(
        gathered, spread, preferred_element_type=F32, precision=lax.Precision.HIGHEST
    )
    for c in range(2):
        total = jnp.zeros((wx, LEVELS), F32)
        for a in range(RX + 2):
            start = (2 * a + c) * wx
            total = total + gathered[start : start + wx] * wanted[a]
        shift = LEVELS // 2
        while shift >= wy:
            total = total + pltpu.roll(total, shift, 1)
            shift //= 2
        current_o[c] = total[:, :wy]


def solution(mesh):
    size_x, size_y = mesh.shape["gx"], mesh.shape["gy"]

    def step(
        spectrum,
        courant,
        source,
        wave_land,
        stokes_kernel,
        velocity,
        coriolis,
        ocean_codes,
        ocean_weights,
        wave_codes,
        wave_weights,
    ):
        wx, wy, bins = spectrum.shape
        ox, oy, levels = velocity.shape
        turn = lambda value: jnp.transpose(value, (0, 2, 1))
        operands = (
            spectrum,
            courant,
            source,
            wave_land,
            stokes_kernel,
            velocity,
            coriolis,
            turn(ocean_codes),
            turn(ocean_weights),
            turn(wave_codes),
            turn(wave_weights),
        )
        vmem = pltpu.VMEM
        edge_x = vmem((2, oy, levels), BF16)
        edge_y = vmem((2, ox, levels), BF16)
        prof_edge = vmem((2, wx, levels), BF16)
        tile = vmem((2, 8, levels), F32)
        copies = 28
        scratch = [
            vmem((wx + 2, wy, bins), BF16),
            vmem((2, bins), F32),
            vmem((wx, wy), F32),
            vmem((wx, wy), jnp.int32),
            vmem((bins, levels), BF16),
            vmem((ox + 4, oy + 16, levels), F32),
            vmem((ox + 4, oy + 16, levels), F32),
            vmem((ox, oy), F32),
            vmem((ox, K, oy), jnp.int32),
            vmem((ox, K, oy), F32),
            vmem((wx, K, wy), jnp.int32),
            vmem((wx, K, wy), F32),
            pltpu.SemaphoreType.DMA((11,)),
            vmem((4, wx, bins), F32),
            vmem((2, wx, bins), BF16),
            vmem((2, wx, bins), BF16),
            vmem((2, wx, bins), F32),
            edge_x,
            edge_x,
            edge_y,
            edge_y,
            edge_x,
            edge_x,
            edge_y,
            edge_y,
            vmem((4 * wx, bins), BF16),
            vmem((wx + 3, PITCH, levels), F32),
            prof_edge,
            prof_edge,
            prof_edge,
            prof_edge,
            prof_edge,
            vmem((4, wx, levels), BF16),
            vmem((wx, levels, 2 * levels), BF16),
            vmem((ox, oy, levels), F32),
            vmem((ox, oy, levels), F32),
            vmem((8, bins), F32),
            vmem((2, ox + 16, levels), F32),
            tile,
            tile,
            tile,
            tile,
            vmem((4, 8, levels), F32),
            pltpu.SemaphoreType.DMA((copies,)),
            pltpu.SemaphoreType.DMA((copies,)),
        ]
        body = lambda *refs: kernel(size_x, size_y, *refs)
        return pl.pallas_call(
            body,
            out_shape=(
                pltpu.VMEM((wx, wy, bins), BF16),
                pltpu.VMEM((ox, oy, levels), F32),
                jax.ShapeDtypeStruct((2, wx, wy), F32),
            ),
            in_specs=[pl.BlockSpec(memory_space=pltpu.HBM)] * len(operands),
            out_specs=(pl.BlockSpec(memory_space=pltpu.VMEM),) * 3,
            scratch_shapes=scratch,
            compiler_params=pltpu.CompilerParams(
                collective_id=0, has_side_effects=True, vmem_limit_bytes=40000000
            ),
            name="coupled_step",
        )(*[pltpu.with_memory_space_constraint(o, pltpu.HBM) for o in operands])

    return jax.shard_map(
        step,
        mesh=mesh,
        in_specs=(
            P("gx", "gy", None),
            P(),
            P("gx", "gy"),
            P("gx", "gy"),
            P(),
            P("gx", "gy", None),
            P("gx", "gy"),
            P("gx", "gy", None),
            P("gx", "gy", None),
            P("gx", "gy", None),
            P("gx", "gy", None),
        ),
        out_specs=(P("gx", "gy", None), P("gx", "gy", None), P(None, "gx", "gy")),
        check_vma=False,
    )
```

```python
import jax
import jax.numpy as jnp
from jax import lax
from jax.experimental import pallas as pl
from jax.experimental.pallas import tpu as pltpu
from jax.sharding import PartitionSpec as P

NL = 64
LEVELS = 2 * NL
K = 4
RX = 2
RY = 4
PITCH = 32
MESH = pl.DeviceIdType.MESH
F32 = jnp.float32
BF16 = jnp.bfloat16

time_step = 0.5


def kernel(
    size_x,
    size_y,
    spectrum_h,
    courant_h,
    source_h,
    land_h,
    stokes_h,
    velocity_h,
    coriolis_h,
    ocodes_h,
    oweights_h,
    wcodes_h,
    wweights_h,
    spectrum_o,
    velocity_o,
    current_o,
    cells,
    courant,
    source,
    land,
    stokes_kernel,
    wide,
    middle,
    coriolis,
    ocodes,
    oweights,
    wcodes,
    wweights,
    load_sem,
    edge_f,
    edge_s,
    edge_r,
    south_north,
    vx_s,
    vx_r,
    vy_s,
    vy_r,
    mx_s,
    mx_r,
    my_s,
    my_r,
    strip,
    prof,
    px_s,
    px_r,
    py_s,
    py_r,
    pd_s,
    pd_r,
    select,
    stokes,
    cor,
    coef,
    means,
    ex_s,
    ex_r,
    ey_s,
    ey_r,
    ed_r,
    send_sem,
    recv_sem,
):
    wx, wy, bins = spectrum_o.shape
    ox, oy = velocity_o.shape[:2]
    ix, iy = lax.axis_index("gx"), lax.axis_index("gy")
    at_south, at_north = iy == 0, iy == size_y - 1

    def peer(dx, dy):
        return (lax.rem(ix + dx + size_x, size_x), lax.rem(iy + dy + size_y, size_y))

    straight = ((-1, 0), (1, 0), (0, -1), (0, 1))
    barrier = pltpu.get_barrier_semaphore()
    for step in straight:
        pl.semaphore_signal(barrier, inc=1, device_id=peer(*step), device_id_type=MESH)

    loads = [
        pltpu.make_async_copy(src, dst, load_sem.at[i])
        for i, (src, dst) in enumerate(
            (
                (spectrum_h, cells.at[pl.ds(1, wx)]),
                (velocity_h, wide.at[pl.ds(2, ox), pl.ds(8, oy)]),
                (ocodes_h, ocodes),
                (oweights_h, oweights),
                (coriolis_h, coriolis),
                (wcodes_h, wcodes),
                (wweights_h, wweights),
                (courant_h, courant),
                (source_h, source),
                (land_h, land),
                (stokes_h, stokes_kernel),
            )
        )
    ]
    for load in loads:
        load.start()

    count = [0]

    def remote(src, dst, step):
        i = count[0]
        count[0] += 1
        return pltpu.make_async_remote_copy(
            src_ref=src,
            dst_ref=dst,
            send_sem=send_sem.at[i],
            recv_sem=recv_sem.at[i],
            device_id=peer(*step),
            device_id_type=MESH,
        )

    lane = lax.broadcasted_iota(jnp.int32, (1, LEVELS), 1)
    low = lane < NL

    def swap(value):
        return pltpu.roll(value, NL, 1)

    def pack_x(ref, side, row):
        edge = jnp.where(low, swap(ref[row, pl.ds(8, oy), :]), ref[row + 1, pl.ds(8, oy), :])
        side[...] = edge.astype(BF16)

    def pack_y(ref, side, col):
        edge = jnp.where(low, ref[pl.ds(2, ox), col, :], swap(ref[pl.ds(2, ox), col + 1, :]))
        side[...] = edge.astype(BF16)

    def unpack_x(ref, side, row):
        edge = side[...].astype(F32)
        ref[row, pl.ds(8, oy), :] = swap(edge)
        ref[row + 1, pl.ds(8, oy), :] = edge

    def unpack_y(ref, side, col, outside):
        edge = side[...].astype(F32)
        edge = jnp.where(outside, jnp.zeros_like(edge), edge)
        ref[pl.ds(2, ox), col, :] = edge
        ref[pl.ds(2, ox), col + 1, :] = swap(edge)

    loads[0].wait()
    for x in range(wx):
        row = cells[x + 1].astype(F32)
        for slot, col in enumerate((0, 1, wy - 2, wy - 1)):
            edge_f[slot, x : x + 1, :] = row[col : col + 1]
    edge_s[0] = edge_f[0].astype(BF16)
    edge_s[1] = edge_f[3].astype(BF16)
    loads[1].wait()
    pack_x(wide, vx_s.at[0], 2)
    pack_x(wide, vx_s.at[1], ox)
    pack_y(wide, vy_s.at[0], 8)
    pack_y(wide, vy_s.at[1], 6 + oy)

    pl.semaphore_wait(barrier, 4)
    first = [
        remote(cells.at[wx], cells.at[0], (1, 0)),
        remote(cells.at[1], cells.at[wx + 1], (-1, 0)),
        remote(edge_s.at[1], edge_r.at[0], (0, 1)),
        remote(edge_s.at[0], edge_r.at[1], (0, -1)),
        remote(vx_s.at[1], vx_r.at[0], (1, 0)),
        remote(vx_s.at[0], vx_r.at[1], (-1, 0)),
        remote(vy_s.at[1], vy_r.at[0], (0, 1)),
        remote(vy_s.at[0], vy_r.at[1], (0, -1)),
    ]
    for copy in first[:4]:
        copy.start()

    for load in loads[2:]:
        load.wait()
    prof[...] = jnp.zeros_like(prof)
    means[...] = jnp.zeros_like(means)
    speed_x, speed_y = courant[0:1, :], courant[1:2, :]
    coef[0:1, :] = 1.0 - jnp.abs(speed_x) - jnp.abs(speed_y)
    coef[1:2, :] = jnp.maximum(speed_x, 0.0)
    coef[2:3, :] = jnp.maximum(-speed_x, 0.0)
    coef[3:4, :] = jnp.maximum(speed_y, 0.0)
    coef[4:5, :] = jnp.maximum(-speed_y, 0.0)

    slot_row = lax.broadcasted_iota(jnp.int32, (LEVELS, LEVELS), 0)
    own_cell = lax.rem(lane, oy) // RY

    @pl.loop(0, wx)
    def _(i):
        def pair(ref, entry):
            return jnp.concatenate(
                [ref[RX * i, entry : entry + 1, :], ref[RX * i + 1, entry : entry + 1, :]], axis=1
            )

        weights = [pair(oweights, entry) for entry in range(K)]
        total = weights[0] + weights[1] + weights[2] + weights[3]
        rows = jnp.zeros((LEVELS, LEVELS), F32)
        for entry in range(K):
            code = pair(ocodes, entry)
            third = lax.shift_right_logical(code * 11, 5)
            slot = third * (PITCH - 3) + code + own_cell
            rows = rows + jnp.where(slot_row == slot, weights[entry] / total, 0.0)
        rows = rows.T
        high = rows.astype(BF16)
        select[i, :, 0:LEVELS] = high
        select[i, :, LEVELS : 2 * LEVELS] = (rows - high.astype(F32)).astype(BF16)

    turned = coriolis[...].T

    @pl.loop(0, ox)
    def _(x):
        here = lax.broadcasted_iota(jnp.int32, (oy, ox), 1) == x
        column = jnp.sum(jnp.where(here, turned, 0.0), axis=1, keepdims=True)
        cor[x] = jnp.broadcast_to(column, (oy, LEVELS))

    for copy in first[:4]:
        copy.wait()
    for side, outside in ((0, at_south), (1, at_north)):
        value = edge_r[side].astype(F32)
        south_north[side] = jnp.where(outside, jnp.zeros_like(value), value)

    growth = land[...].astype(F32)
    gain_rows = growth * (1.0 + 0.2 * source[...])
    damp_rows = 0.1 * growth
    gain, damp = gain_rows.T, damp_rows.T
    chunk = 3 * LEVELS
    cell_x = lax.broadcasted_iota(jnp.int32, (wx, chunk), 0)
    cell_y = lax.broadcasted_iota(jnp.int32, (wy, chunk), 0)

    def updated(span, center, west, east, south, north, gain_x, damp_x):
        advected = (
            coef[0:1, span] * center
            + coef[1:2, span] * west
            + coef[2:3, span] * east
            + coef[3:4, span] * south
            + coef[4:5, span] * north
        )
        return (advected * (gain_x - damp_x * advected)).astype(BF16)

    def update_row(x):
        here = lax.broadcasted_iota(jnp.int32, (wy, wx), 1) == x
        gain_x = jnp.sum(jnp.where(here, gain, 0.0), axis=1, keepdims=True)
        damp_x = jnp.sum(jnp.where(here, damp, 0.0), axis=1, keepdims=True)
        for start in range(0, bins, chunk):
            span = pl.ds(start, chunk)
            center = cells[x + 1, :, span].astype(F32)
            south = jnp.where(cell_y == 0, south_north[0, pl.ds(x, 1), span], pltpu.roll(center, 1, 0))
            north = jnp.where(
                cell_y == wy - 1, south_north[1, pl.ds(x, 1), span], pltpu.roll(center, wy - 1, 0)
            )
            west, east = cells[x, :, span].astype(F32), cells[x + 2, :, span].astype(F32)
            spectrum_o[x, :, span] = updated(span, center, west, east, south, north, gain_x, damp_x)

    def as_profile(value):
        value = jnp.dot(value, stokes_kernel[...], preferred_element_type=F32)
        value = value.astype(BF16).astype(F32)
        return jnp.where(low, swap(value), -swap(value))

    update_row(0)
    update_row(wx - 1)
    strip[0:wx] = spectrum_o[0]
    strip[wx : 2 * wx] = spectrum_o[wx - 1]
    for side, col in ((0, 0), (1, wy - 1)):
        for start in range(0, bins, chunk):
            span = pl.ds(start, chunk)
            center = edge_f[3 * side, :, span]
            before = cells[0, :, span].astype(F32)[col : col + 1]
            after = cells[wx + 1, :, span].astype(F32)[col : col + 1]
            west = jnp.where(cell_x == 0, before, pltpu.roll(center, 1, 0))
            east = jnp.where(cell_x == wx - 1, after, pltpu.roll(center, wx - 1, 0))
            inner, outer = edge_f[1 + side, :, span], south_north[side, :, span]
            south, north = (inner, outer) if side else (outer, inner)
            strip[(2 + side) * wx : (3 + side) * wx, span] = updated(
                span, center, west, east, south, north,
                gain_rows[:, col : col + 1], damp_rows[:, col : col + 1],
            )
    outermost = as_profile(strip[...]).astype(BF16)
    px_s[0] = outermost[0:wx]
    px_s[1] = outermost[wx : 2 * wx]
    py_s[0] = outermost[2 * wx : 3 * wx]
    py_s[1] = outermost[3 * wx : 4 * wx]
    second = [
        remote(px_s.at[1], px_r.at[0], (1, 0)),
        remote(px_s.at[0], px_r.at[1], (-1, 0)),
        remote(py_s.at[1], py_r.at[0], (0, 1)),
        remote(py_s.at[0], py_r.at[1], (0, -1)),
        remote(px_s.at[1], pd_r.at[0], (1, 1)),
        remote(px_s.at[1], pd_r.at[1], (1, -1)),
        remote(px_s.at[0], pd_r.at[2], (-1, 1)),
        remote(px_s.at[0], pd_r.at[3], (-1, -1)),
    ]
    for copy in second + first[4:]:
        copy.start()

    @pl.loop(1, wx - 1)
    def _(x):
        update_row(x)

    own = as_profile(spectrum_o[...].reshape(wx * wy, bins))
    prof[pl.ds(1, wx), pl.ds(1, wy), :] = own.reshape(wx, wy, LEVELS)
    for copy in first[4:]:
        copy.wait()
    unpack_x(wide, vx_r.at[0], 0)
    unpack_x(wide, vx_r.at[1], ox + 2)
    unpack_y(wide, vy_r.at[0], 6, at_south)
    unpack_y(wide, vy_r.at[1], 8 + oy, at_north)
    for copy in second:
        copy.wait()
    prof[0, pl.ds(1, wy), :] = px_r[0].astype(F32)
    prof[wx + 1, pl.ds(1, wy), :] = px_r[1].astype(F32)
    for side, outside, col in ((0, at_south, 0), (1, at_north, wy + 1)):
        value = py_r[side].astype(F32)
        prof[pl.ds(1, wx), col, :] = jnp.where(outside, jnp.zeros_like(value), value)
    for i, row, col, outside, line in (
        (0, 0, 0, at_south, wy - 1),
        (1, 0, wy + 1, at_north, 0),
        (2, wx + 1, 0, at_south, wy - 1),
        (3, wx + 1, wy + 1, at_north, 0),
    ):
        value = pd_r[i].astype(F32)[line : line + 1]
        prof[row, col : col + 1, :] = jnp.where(outside, jnp.zeros_like(value), value)

    c1 = jnp.where(low, -8.0 / 12.0, 8.0 / 12.0)
    c2 = jnp.where(low, -1.0 / 12.0, 1.0 / 12.0)

    def block(ref, x, rows, y, cols):
        return ref[pl.ds(x + 2, rows), pl.ds(y + 8, cols), :]

    def absolute(ref, x, rows, y, cols):
        def ahead(step):
            return jnp.where(
                low, block(ref, x, rows, y + step, cols), block(ref, x + step, rows, y, cols)
            )

        turn = c1 * (ahead(1) - ahead(-1)) - c2 * (ahead(2) - ahead(-2))
        return cor[pl.ds(x, rows), pl.ds(y, cols), :] + turn + pltpu.roll(turn, NL, 2)

    def advance(x, rows, y, cols):
        drift = stokes[pl.ds(x, rows), pl.ds(y, cols), :]
        middle[pl.ds(x + 2, rows), pl.ds(y + 8, cols), :] = (
            block(wide, x, rows, y, cols) + time_step * absolute(wide, x, rows, y, cols) * drift
        )

    @pl.loop(0, wx // 8)
    def _(group):
        for part in range(8):
            i = 8 * group + part
            near = prof[pl.ds(i, 4)].reshape(4 * PITCH, LEVELS).astype(BF16)
            near = jnp.concatenate([near, near], axis=0)
            both = jnp.dot(select[i], near, preferred_element_type=F32)
            stokes[pl.ds(RX * i, RX)] = both.reshape(RX, oy, LEVELS)

    advance(0, 2, 0, oy)
    advance(ox - 2, 2, 0, oy)

    for i in range(0, ox, 8):
        advance(i, 8, 0, 8)
        advance(i, 8, oy - 8, 8)

    pack_x(middle, mx_s.at[0], 2)
    pack_x(middle, mx_s.at[1], ox)
    pack_y(middle, my_s.at[0], 8)
    pack_y(middle, my_s.at[1], 6 + oy)
    third = [
        remote(mx_s.at[1], mx_r.at[0], (1, 0)),
        remote(mx_s.at[0], mx_r.at[1], (-1, 0)),
        remote(my_s.at[1], my_r.at[0], (0, 1)),
        remote(my_s.at[0], my_r.at[1], (0, -1)),
    ]
    for copy in third:
        copy.start()

    @pl.loop(0, wx)
    def _(i):
        advance(RX * i, RX, 8, oy - 16)

    target = lax.broadcasted_iota(jnp.int32, (LEVELS, LEVELS), 1)
    origin = lax.broadcasted_iota(jnp.int32, (LEVELS, LEVELS), 0)
    offset = RY * lax.rem(target, wy) + target // wy - 1
    used = lane < (RY + 2) * wy
    spread = jnp.where((origin == (offset & (LEVELS - 1))) & used, 1.0, 0.0)
    repeat = LEVELS // wy
    wave_sum = wweights[:, 0, :] + wweights[:, 1, :] + wweights[:, 2, :] + wweights[:, 3, :]
    tiled = [
        (
            jnp.concatenate([wcodes[:, entry, :]] * repeat, axis=1),
            jnp.concatenate([wweights[:, entry, :] / wave_sum] * repeat, axis=1),
        )
        for entry in range(K)
    ]
    wanted = []
    for a in range(RX + 2):
        number = (RY + 2) * a + lane // wy
        chosen = jnp.zeros((wx, LEVELS), F32)
        for code, weight in tiled:
            chosen = chosen + jnp.where((code == number) & used, weight, 0.0)
        wanted.append(chosen)

    for copy in third:
        copy.wait()
    unpack_x(middle, mx_r.at[0], 0)
    unpack_x(middle, mx_r.at[1], ox + 2)
    unpack_y(middle, my_r.at[0], 6, at_south)
    unpack_y(middle, my_r.at[1], 8 + oy, at_north)

    def finish(x, rows, y, cols):
        rate = absolute(middle, x, rows, y, cols) * stokes[pl.ds(x, rows), pl.ds(y, cols), :]
        old = block(wide, x, rows, y, cols) + block(middle, x, rows, y, cols)
        value = 0.5 * old + (0.5 * time_step) * rate
        velocity_o[pl.ds(x, rows), pl.ds(y, cols), :] = value
        mean_u = jnp.sum(jnp.where(low, value, 0.0), axis=2, keepdims=True)
        mean_v = jnp.sum(jnp.where(low, 0.0, value), axis=2, keepdims=True)
        return mean_u * (1.0 / NL), mean_v * (1.0 / NL)

    def finish_into(table, x, rows, y, cols):
        mean_u, mean_v = finish(x, rows, y, cols)
        for row in range(rows):
            table = jnp.where(lane == x + row, mean_u[row], table)
            table = jnp.where(lane == x + row + NL, mean_v[row], table)
        return table

    ends = jnp.zeros((oy, LEVELS), F32)
    for side, x in ((0, 0), (1, ox - 1)):
        mean_u, mean_v = finish(x, 1, 0, oy)
        ends = jnp.where(lane == 2 * side, mean_u[0], ends)
        ends = jnp.where(lane == 2 * side + 1, mean_v[0], ends)
    ends = jnp.concatenate([ends, jnp.zeros((LEVELS - oy, LEVELS), F32)], axis=0).T
    ex_s[0, 0:2, :] = ends[0:2]
    ex_s[1, 0:2, :] = ends[2:4]

    first_cols = last_cols = jnp.zeros((8, LEVELS), F32)
    for i in range(0, ox, 8):
        first_cols = finish_into(first_cols, i, 8, 0, 8)
        last_cols = finish_into(last_cols, i, 8, oy - 8, 8)
    ey_s[0] = first_cols
    ey_s[1] = last_cols
    fourth = [
        remote(ex_s.at[1], ex_r.at[0], (1, 0)),
        remote(ex_s.at[0], ex_r.at[1], (-1, 0)),
        remote(ey_s.at[1], ey_r.at[0], (0, 1)),
        remote(ey_s.at[0], ey_r.at[1], (0, -1)),
        remote(ey_s.at[1], ed_r.at[0], (1, 1)),
        remote(ey_s.at[0], ed_r.at[1], (1, -1)),
        remote(ey_s.at[1], ed_r.at[2], (-1, 1)),
        remote(ey_s.at[0], ed_r.at[3], (-1, -1)),
    ]
    for copy in fourth:
        copy.start()

    inner_cols = lax.fori_loop(
        0,
        wx,
        lambda i, table: finish_into(table, RX * i, RX, 8, oy - 16),
        jnp.zeros((oy - 16, LEVELS), F32),
    )
    blank = jnp.zeros((LEVELS - oy, LEVELS), F32)
    by_row = jnp.concatenate([first_cols, inner_cols, last_cols, blank], axis=0).T
    for c in range(2):
        means[c, pl.ds(8, ox), :] = by_row[c * NL : c * NL + ox]

    for copy in fourth:
        copy.wait()
    for c in range(2):
        means[c, 7:8, :] = ex_r[0, c : c + 1, :]
        means[c, 8 + ox : 9 + ox, :] = ex_r[1, c : c + 1, :]
    for side, line, outside, spot, near in (
        (0, 7, at_south, LEVELS - 1, (0, 2)),
        (1, 0, at_north, oy, (1, 3)),
    ):
        here = lane == spot
        column = ey_r[side].T[:, line : line + 1]
        for c in range(2):
            inner = column[c * NL : c * NL + ox]
            inner = jnp.where(outside, jnp.zeros_like(inner), inner)
            means[c, pl.ds(8, ox), :] = jnp.where(here, inner, means[c, pl.ds(8, ox), :])
            for index, row, source_x in ((near[0], 7, ox - 1), (near[1], 8 + ox, 0)):
                spot_x = c * NL + source_x
                corner = ed_r[index, line : line + 1, spot_x : spot_x + 1]
                corner = jnp.where(outside, jnp.zeros_like(corner), corner)
                means[c, row : row + 1, :] = jnp.where(here, corner, means[c, row : row + 1, :])

    gathered = jnp.concatenate(
        [means[c, pl.ds(7 + a, wx, stride=RX), :] for a in range(RX + 2) for c in range(2)], axis=0
    )
    gathered = jnp.dot(
        gathered, spread, preferred_element_type=F32, precision=lax.Precision.HIGHEST
    )
    for c in range(2):
        total = jnp.zeros((wx, LEVELS), F32)
        for a in range(RX + 2):
            start = (2 * a + c) * wx
            total = total + gathered[start : start + wx] * wanted[a]
        shift = LEVELS // 2
        while shift >= wy:
            total = total + pltpu.roll(total, shift, 1)
            shift //= 2
        current_o[c] = total[:, :wy]


def store(*refs):
    sources, targets, sems = refs[:3], refs[3:6], refs[6]
    copies = [
        pltpu.make_async_copy(source, target, sems.at[i])
        for i, (source, target) in enumerate(zip(sources, targets))
    ]
    for copy in copies:
        copy.start()
    for copy in copies:
        copy.wait()


def solution(mesh):
    size_x, size_y = mesh.shape["gx"], mesh.shape["gy"]

    def step(
        spectrum,
        courant,
        source,
        wave_land,
        stokes_kernel,
        velocity,
        coriolis,
        ocean_codes,
        ocean_weights,
        wave_codes,
        wave_weights,
    ):
        wx, wy, bins = spectrum.shape
        ox, oy, levels = velocity.shape
        turn = lambda value: jnp.transpose(value, (0, 2, 1))
        operands = (
            spectrum,
            courant,
            source,
            wave_land,
            stokes_kernel,
            velocity,
            coriolis,
            turn(ocean_codes),
            turn(ocean_weights),
            turn(wave_codes),
            turn(wave_weights),
        )
        vmem = pltpu.VMEM
        edge_x = vmem((2, oy, levels), BF16)
        edge_y = vmem((2, ox, levels), BF16)
        prof_edge = vmem((2, wx, levels), BF16)
        tile = vmem((2, 8, levels), F32)
        copies = 28
        scratch = [
            vmem((wx + 2, wy, bins), BF16),
            vmem((2, bins), F32),
            vmem((wx, wy), F32),
            vmem((wx, wy), jnp.int32),
            vmem((bins, levels), BF16),
            vmem((ox + 4, oy + 16, levels), F32),
            vmem((ox + 4, oy + 16, levels), F32),
            vmem((ox, oy), F32),
            vmem((ox, K, oy), jnp.int32),
            vmem((ox, K, oy), F32),
            vmem((wx, K, wy), jnp.int32),
            vmem((wx, K, wy), F32),
            pltpu.SemaphoreType.DMA((11,)),
            vmem((4, wx, bins), F32),
            vmem((2, wx, bins), BF16),
            vmem((2, wx, bins), BF16),
            vmem((2, wx, bins), F32),
            edge_x,
            edge_x,
            edge_y,
            edge_y,
            edge_x,
            edge_x,
            edge_y,
            edge_y,
            vmem((4 * wx, bins), BF16),
            vmem((wx + 3, PITCH, levels), F32),
            prof_edge,
            prof_edge,
            prof_edge,
            prof_edge,
            prof_edge,
            vmem((4, wx, levels), BF16),
            vmem((wx, levels, 2 * levels), BF16),
            vmem((ox, oy, levels), F32),
            vmem((ox, oy, levels), F32),
            vmem((8, bins), F32),
            vmem((2, ox + 16, levels), F32),
            tile,
            tile,
            tile,
            tile,
            vmem((4, 8, levels), F32),
            pltpu.SemaphoreType.DMA((copies,)),
            pltpu.SemaphoreType.DMA((copies,)),
        ]
        body = lambda *refs: kernel(size_x, size_y, *refs)
        results = pl.pallas_call(
            body,
            out_shape=(
                pltpu.VMEM((wx, wy, bins), BF16),
                pltpu.VMEM((ox, oy, levels), F32),
                pltpu.VMEM((2, wx, wy), F32),
            ),
            in_specs=[pl.BlockSpec(memory_space=pltpu.HBM)] * len(operands),
            out_specs=(pl.BlockSpec(memory_space=pltpu.VMEM),) * 3,
            scratch_shapes=scratch,
            compiler_params=pltpu.CompilerParams(
                collective_id=0, has_side_effects=True, vmem_limit_bytes=40000000
            ),
            name="coupled_step",
        )(*[pltpu.with_memory_space_constraint(o, pltpu.HBM) for o in operands])
        return pl.pallas_call(
            store,
            out_shape=tuple(jax.ShapeDtypeStruct(r.shape, r.dtype) for r in results),
            in_specs=[pl.BlockSpec(memory_space=pltpu.VMEM)] * 3,
            out_specs=(pl.BlockSpec(memory_space=pltpu.HBM),) * 3,
            scratch_shapes=[pltpu.SemaphoreType.DMA((3,))],
            compiler_params=pltpu.CompilerParams(vmem_limit_bytes=40000000),
            name="store_results",
        )(*[pltpu.with_memory_space_constraint(r, pltpu.VMEM) for r in results])

    return jax.shard_map(
        step,
        mesh=mesh,
        in_specs=(
            P("gx", "gy", None),
            P(),
            P("gx", "gy"),
            P("gx", "gy"),
            P(),
            P("gx", "gy", None),
            P("gx", "gy"),
            P("gx", "gy", None),
            P("gx", "gy", None),
            P("gx", "gy", None),
            P("gx", "gy", None),
        ),
        out_specs=(P("gx", "gy", None), P("gx", "gy", None), P(None, "gx", "gy")),
        check_vma=False,
    )
```

```python
import jax
import jax.numpy as jnp
from jax import lax
from jax.experimental import pallas as pl
from jax.experimental.pallas import tpu as pltpu
from jax.sharding import PartitionSpec as P

NL = 64
LEVELS = 2 * NL
K = 4
RX = 2
RY = 4
PITCH = 32
MESH = pl.DeviceIdType.MESH
F32 = jnp.float32
BF16 = jnp.bfloat16

time_step = 0.5


def kernel(
    size_x,
    size_y,
    spectrum_h,
    courant_h,
    source_h,
    land_h,
    stokes_h,
    velocity_h,
    coriolis_h,
    ocodes_h,
    oweights_h,
    wcodes_h,
    wweights_h,
    spectrum_o,
    velocity_o,
    current_o,
    cells,
    courant,
    source,
    land,
    stokes_kernel,
    wide,
    middle,
    coriolis,
    ocodes,
    oweights,
    wcodes,
    wweights,
    load_sem,
    edge_f,
    edge_s,
    edge_r,
    south_north,
    vx_s,
    vx_r,
    vy_s,
    vy_r,
    mx_s,
    mx_r,
    my_s,
    my_r,
    strip,
    prof,
    px_s,
    px_r,
    py_s,
    py_r,
    pd_s,
    pd_r,
    select,
    stokes,
    cor,
    coef,
    means,
    ex_s,
    ex_r,
    ey_s,
    ey_r,
    ed_r,
    send_sem,
    recv_sem,
):
    wx, wy, bins = spectrum_o.shape
    ox, oy = velocity_o.shape[:2]
    ix, iy = lax.axis_index("gx"), lax.axis_index("gy")
    at_south, at_north = iy == 0, iy == size_y - 1

    def peer(dx, dy):
        return (lax.rem(ix + dx + size_x, size_x), lax.rem(iy + dy + size_y, size_y))

    straight = ((-1, 0), (1, 0), (0, -1), (0, 1))
    barrier = pltpu.get_barrier_semaphore()
    for step in straight:
        pl.semaphore_signal(barrier, inc=1, device_id=peer(*step), device_id_type=MESH)

    loads = [
        pltpu.make_async_copy(src, dst, load_sem.at[i])
        for i, (src, dst) in enumerate(
            (
                (spectrum_h, cells.at[pl.ds(1, wx)]),
                (velocity_h, wide.at[pl.ds(2, ox), pl.ds(8, oy)]),
                (ocodes_h, ocodes),
                (oweights_h, oweights),
                (coriolis_h, coriolis),
                (wcodes_h, wcodes),
                (wweights_h, wweights),
                (courant_h, courant),
                (source_h, source),
                (land_h, land),
                (stokes_h, stokes_kernel),
            )
        )
    ]
    for load in loads:
        load.start()

    count = [0]

    def remote(src, dst, step):
        i = count[0]
        count[0] += 1
        return pltpu.make_async_remote_copy(
            src_ref=src,
            dst_ref=dst,
            send_sem=send_sem.at[i],
            recv_sem=recv_sem.at[i],
            device_id=peer(*step),
            device_id_type=MESH,
        )

    lane = lax.broadcasted_iota(jnp.int32, (1, LEVELS), 1)
    low = lane < NL

    def swap(value):
        return pltpu.roll(value, NL, 1)

    def pack_x(ref, side, row):
        edge = jnp.where(low, swap(ref[row, pl.ds(8, oy), :]), ref[row + 1, pl.ds(8, oy), :])
        side[...] = edge.astype(BF16)

    def pack_y(ref, side, col):
        edge = jnp.where(low, ref[pl.ds(2, ox), col, :], swap(ref[pl.ds(2, ox), col + 1, :]))
        side[...] = edge.astype(BF16)

    def unpack_x(ref, side, row):
        edge = side[...].astype(F32)
        ref[row, pl.ds(8, oy), :] = swap(edge)
        ref[row + 1, pl.ds(8, oy), :] = edge

    def unpack_y(ref, side, col, outside):
        edge = side[...].astype(F32)
        edge = jnp.where(outside, jnp.zeros_like(edge), edge)
        ref[pl.ds(2, ox), col, :] = edge
        ref[pl.ds(2, ox), col + 1, :] = swap(edge)

    loads[0].wait()
    for x in range(wx):
        row = cells[x + 1].astype(F32)
        for slot, col in enumerate((0, 1, wy - 2, wy - 1)):
            edge_f[slot, x : x + 1, :] = row[col : col + 1]
    edge_s[0] = edge_f[0].astype(BF16)
    edge_s[1] = edge_f[3].astype(BF16)
    loads[1].wait()
    pack_x(wide, vx_s.at[0], 2)
    pack_x(wide, vx_s.at[1], ox)
    pack_y(wide, vy_s.at[0], 8)
    pack_y(wide, vy_s.at[1], 6 + oy)

    pl.semaphore_wait(barrier, 4)
    first = [
        remote(cells.at[wx], cells.at[0], (1, 0)),
        remote(cells.at[1], cells.at[wx + 1], (-1, 0)),
        remote(edge_s.at[1], edge_r.at[0], (0, 1)),
        remote(edge_s.at[0], edge_r.at[1], (0, -1)),
        remote(vx_s.at[1], vx_r.at[0], (1, 0)),
        remote(vx_s.at[0], vx_r.at[1], (-1, 0)),
        remote(vy_s.at[1], vy_r.at[0], (0, 1)),
        remote(vy_s.at[0], vy_r.at[1], (0, -1)),
    ]
    for copy in first[:4]:
        copy.start()

    for load in loads[2:]:
        load.wait()
    prof[...] = jnp.zeros_like(prof)
    means[...] = jnp.zeros_like(means)
    speed_x, speed_y = courant[0:1, :], courant[1:2, :]
    coef[0:1, :] = 1.0 - jnp.abs(speed_x) - jnp.abs(speed_y)
    coef[1:2, :] = jnp.maximum(speed_x, 0.0)
    coef[2:3, :] = jnp.maximum(-speed_x, 0.0)
    coef[3:4, :] = jnp.maximum(speed_y, 0.0)
    coef[4:5, :] = jnp.maximum(-speed_y, 0.0)

    slot_row = lax.broadcasted_iota(jnp.int32, (LEVELS, LEVELS), 0)
    own_cell = lax.rem(lane, oy) // RY

    @pl.loop(0, wx)
    def _(i):
        def pair(ref, entry):
            return jnp.concatenate(
                [ref[RX * i, entry : entry + 1, :], ref[RX * i + 1, entry : entry + 1, :]], axis=1
            )

        weights = [pair(oweights, entry) for entry in range(K)]
        total = weights[0] + weights[1] + weights[2] + weights[3]
        rows = jnp.zeros((LEVELS, LEVELS), F32)
        for entry in range(K):
            code = pair(ocodes, entry)
            third = lax.shift_right_logical(code * 11, 5)
            slot = third * (PITCH - 3) + code + own_cell
            rows = rows + jnp.where(slot_row == slot, weights[entry] / total, 0.0)
        rows = rows.T
        high = rows.astype(BF16)
        select[i, :, 0:LEVELS] = high
        select[i, :, LEVELS : 2 * LEVELS] = (rows - high.astype(F32)).astype(BF16)

    turned = coriolis[...].T

    @pl.loop(0, ox)
    def _(x):
        here = lax.broadcasted_iota(jnp.int32, (oy, ox), 1) == x
        column = jnp.sum(jnp.where(here, turned, 0.0), axis=1, keepdims=True)
        cor[x] = jnp.broadcast_to(column, (oy, LEVELS))

    for copy in first[:4]:
        copy.wait()
    for side, outside in ((0, at_south), (1, at_north)):
        value = edge_r[side].astype(F32)
        south_north[side] = jnp.where(outside, jnp.zeros_like(value), value)

    growth = land[...].astype(F32)
    gain_rows = growth * (1.0 + 0.2 * source[...])
    damp_rows = 0.1 * growth
    gain, damp = gain_rows.T, damp_rows.T
    chunk = 3 * LEVELS
    cell_x = lax.broadcasted_iota(jnp.int32, (wx, chunk), 0)
    cell_y = lax.broadcasted_iota(jnp.int32, (wy, chunk), 0)

    def updated(span, center, west, east, south, north, gain_x, damp_x):
        advected = (
            coef[0:1, span] * center
            + coef[1:2, span] * west
            + coef[2:3, span] * east
            + coef[3:4, span] * south
            + coef[4:5, span] * north
        )
        return (advected * (gain_x - damp_x * advected)).astype(BF16)

    def update_row(x):
        here = lax.broadcasted_iota(jnp.int32, (wy, wx), 1) == x
        gain_x = jnp.sum(jnp.where(here, gain, 0.0), axis=1, keepdims=True)
        damp_x = jnp.sum(jnp.where(here, damp, 0.0), axis=1, keepdims=True)
        for start in range(0, bins, chunk):
            span = pl.ds(start, chunk)
            center = cells[x + 1, :, span].astype(F32)
            south = jnp.where(cell_y == 0, south_north[0, pl.ds(x, 1), span], pltpu.roll(center, 1, 0))
            north = jnp.where(
                cell_y == wy - 1, south_north[1, pl.ds(x, 1), span], pltpu.roll(center, wy - 1, 0)
            )
            west, east = cells[x, :, span].astype(F32), cells[x + 2, :, span].astype(F32)
            spectrum_o[x, :, span] = updated(span, center, west, east, south, north, gain_x, damp_x)

    def as_profile(value):
        value = jnp.dot(value, stokes_kernel[...], preferred_element_type=F32)
        value = value.astype(BF16).astype(F32)
        return jnp.where(low, swap(value), -swap(value))

    update_row(0)
    update_row(wx - 1)
    strip[0:wx] = spectrum_o[0]
    strip[wx : 2 * wx] = spectrum_o[wx - 1]
    second = [
        remote(px_s.at[1], px_r.at[0], (1, 0)),
        remote(px_s.at[0], px_r.at[1], (-1, 0)),
        remote(py_s.at[1], py_r.at[0], (0, 1)),
        remote(py_s.at[0], py_r.at[1], (0, -1)),
        remote(px_s.at[1], pd_r.at[0], (1, 1)),
        remote(px_s.at[1], pd_r.at[1], (1, -1)),
        remote(px_s.at[0], pd_r.at[2], (-1, 1)),
        remote(px_s.at[0], pd_r.at[3], (-1, -1)),
    ]
    outermost = as_profile(strip[0 : 2 * wx]).astype(BF16)
    px_s[0] = outermost[0:wx]
    px_s[1] = outermost[wx : 2 * wx]
    for copy in second[4:] + second[:2]:
        copy.start()
    for side, col in ((0, 0), (1, wy - 1)):
        for start in range(0, bins, chunk):
            span = pl.ds(start, chunk)
            center = edge_f[3 * side, :, span]
            before = cells[0, :, span].astype(F32)[col : col + 1]
            after = cells[wx + 1, :, span].astype(F32)[col : col + 1]
            west = jnp.where(cell_x == 0, before, pltpu.roll(center, 1, 0))
            east = jnp.where(cell_x == wx - 1, after, pltpu.roll(center, wx - 1, 0))
            inner, outer = edge_f[1 + side, :, span], south_north[side, :, span]
            south, north = (inner, outer) if side else (outer, inner)
            strip[(2 + side) * wx : (3 + side) * wx, span] = updated(
                span, center, west, east, south, north,
                gain_rows[:, col : col + 1], damp_rows[:, col : col + 1],
            )
    outermost = as_profile(strip[2 * wx : 4 * wx]).astype(BF16)
    py_s[0] = outermost[0:wx]
    py_s[1] = outermost[wx : 2 * wx]
    for copy in second[2:4] + first[4:]:
        copy.start()

    @pl.loop(1, wx - 1)
    def _(x):
        update_row(x)

    own = as_profile(spectrum_o[...].reshape(wx * wy, bins))
    prof[pl.ds(1, wx), pl.ds(1, wy), :] = own.reshape(wx, wy, LEVELS)
    for copy in first[4:]:
        copy.wait()
    unpack_x(wide, vx_r.at[0], 0)
    unpack_x(wide, vx_r.at[1], ox + 2)
    unpack_y(wide, vy_r.at[0], 6, at_south)
    unpack_y(wide, vy_r.at[1], 8 + oy, at_north)
    for copy in second:
        copy.wait()
    prof[0, pl.ds(1, wy), :] = px_r[0].astype(F32)
    prof[wx + 1, pl.ds(1, wy), :] = px_r[1].astype(F32)
    for side, outside, col in ((0, at_south, 0), (1, at_north, wy + 1)):
        value = py_r[side].astype(F32)
        prof[pl.ds(1, wx), col, :] = jnp.where(outside, jnp.zeros_like(value), value)
    for i, row, col, outside, line in (
        (0, 0, 0, at_south, wy - 1),
        (1, 0, wy + 1, at_north, 0),
        (2, wx + 1, 0, at_south, wy - 1),
        (3, wx + 1, wy + 1, at_north, 0),
    ):
        value = pd_r[i].astype(F32)[line : line + 1]
        prof[row, col : col + 1, :] = jnp.where(outside, jnp.zeros_like(value), value)

    c1 = jnp.where(low, -8.0 / 12.0, 8.0 / 12.0)
    c2 = jnp.where(low, -1.0 / 12.0, 1.0 / 12.0)

    def block(ref, x, rows, y, cols):
        return ref[pl.ds(x + 2, rows), pl.ds(y + 8, cols), :]

    def absolute(ref, x, rows, y, cols):
        def ahead(step):
            return jnp.where(
                low, block(ref, x, rows, y + step, cols), block(ref, x + step, rows, y, cols)
            )

        turn = c1 * (ahead(1) - ahead(-1)) - c2 * (ahead(2) - ahead(-2))
        return cor[pl.ds(x, rows), pl.ds(y, cols), :] + turn + pltpu.roll(turn, NL, 2)

    def advance(x, rows, y, cols):
        drift = stokes[pl.ds(x, rows), pl.ds(y, cols), :]
        middle[pl.ds(x + 2, rows), pl.ds(y + 8, cols), :] = (
            block(wide, x, rows, y, cols) + time_step * absolute(wide, x, rows, y, cols) * drift
        )

    @pl.loop(0, wx // 8)
    def _(group):
        for part in range(8):
            i = 8 * group + part
            near = prof[pl.ds(i, 4)].reshape(4 * PITCH, LEVELS).astype(BF16)
            near = jnp.concatenate([near, near], axis=0)
            both = jnp.dot(select[i], near, preferred_element_type=F32)
            stokes[pl.ds(RX * i, RX)] = both.reshape(RX, oy, LEVELS)

    advance(0, 2, 0, oy)
    advance(ox - 2, 2, 0, oy)
    pack_x(middle, mx_s.at[0], 2)
    pack_x(middle, mx_s.at[1], ox)
    third = [
        remote(mx_s.at[1], mx_r.at[0], (1, 0)),
        remote(mx_s.at[0], mx_r.at[1], (-1, 0)),
        remote(my_s.at[1], my_r.at[0], (0, 1)),
        remote(my_s.at[0], my_r.at[1], (0, -1)),
    ]
    for copy in third[:2]:
        copy.start()

    for i in range(0, ox, 8):
        advance(i, 8, 0, 8)
        advance(i, 8, oy - 8, 8)

    pack_y(middle, my_s.at[0], 8)
    pack_y(middle, my_s.at[1], 6 + oy)
    for copy in third[2:]:
        copy.start()

    @pl.loop(0, wx)
    def _(i):
        advance(RX * i, RX, 8, oy - 16)

    def finish(x, rows, y, cols):
        rate = absolute(middle, x, rows, y, cols) * stokes[pl.ds(x, rows), pl.ds(y, cols), :]
        old = block(wide, x, rows, y, cols) + block(middle, x, rows, y, cols)
        value = 0.5 * old + (0.5 * time_step) * rate
        velocity_o[pl.ds(x, rows), pl.ds(y, cols), :] = value
        mean_u = jnp.sum(jnp.where(low, value, 0.0), axis=2, keepdims=True)
        mean_v = jnp.sum(jnp.where(low, 0.0, value), axis=2, keepdims=True)
        return mean_u * (1.0 / NL), mean_v * (1.0 / NL)

    def finish_into(table, x, rows, y, cols):
        mean_u, mean_v = finish(x, rows, y, cols)
        for row in range(rows):
            table = jnp.where(lane == x + row, mean_u[row], table)
            table = jnp.where(lane == x + row + NL, mean_v[row], table)
        return table

    inner_cols = lax.fori_loop(
        1,
        wx - 1,
        lambda i, table: finish_into(table, RX * i, RX, 8, oy - 16),
        jnp.zeros((oy - 16, LEVELS), F32),
    )

    target = lax.broadcasted_iota(jnp.int32, (LEVELS, LEVELS), 1)
    origin = lax.broadcasted_iota(jnp.int32, (LEVELS, LEVELS), 0)
    offset = RY * lax.rem(target, wy) + target // wy - 1
    used = lane < (RY + 2) * wy
    spread = jnp.where((origin == (offset & (LEVELS - 1))) & used, 1.0, 0.0)
    repeat = LEVELS // wy
    wave_sum = wweights[:, 0, :] + wweights[:, 1, :] + wweights[:, 2, :] + wweights[:, 3, :]
    tiled = [
        (
            jnp.concatenate([wcodes[:, entry, :]] * repeat, axis=1),
            jnp.concatenate([wweights[:, entry, :] / wave_sum] * repeat, axis=1),
        )
        for entry in range(K)
    ]
    wanted = []
    for a in range(RX + 2):
        number = (RY + 2) * a + lane // wy
        chosen = jnp.zeros((wx, LEVELS), F32)
        for code, weight in tiled:
            chosen = chosen + jnp.where((code == number) & used, weight, 0.0)
        wanted.append(chosen)

    for copy in third:
        copy.wait()
    unpack_x(middle, mx_r.at[0], 0)
    unpack_x(middle, mx_r.at[1], ox + 2)
    unpack_y(middle, my_r.at[0], 6, at_south)
    unpack_y(middle, my_r.at[1], 8 + oy, at_north)

    first_cols = last_cols = jnp.zeros((8, LEVELS), F32)
    for i in range(0, ox, 8):
        first_cols = finish_into(first_cols, i, 8, 0, 8)
        last_cols = finish_into(last_cols, i, 8, oy - 8, 8)
    ey_s[0] = first_cols
    ey_s[1] = last_cols
    fourth = [
        remote(ex_s.at[1], ex_r.at[0], (1, 0)),
        remote(ex_s.at[0], ex_r.at[1], (-1, 0)),
        remote(ey_s.at[1], ey_r.at[0], (0, 1)),
        remote(ey_s.at[0], ey_r.at[1], (0, -1)),
        remote(ey_s.at[1], ed_r.at[0], (1, 1)),
        remote(ey_s.at[0], ed_r.at[1], (1, -1)),
        remote(ey_s.at[1], ed_r.at[2], (-1, 1)),
        remote(ey_s.at[0], ed_r.at[3], (-1, -1)),
    ]
    for copy in fourth[4:] + fourth[2:4]:
        copy.start()
    ends = jnp.zeros((oy, LEVELS), F32)
    for side, x in ((0, 0), (1, ox - 1)):
        mean_u, mean_v = finish(x, 1, 0, oy)
        ends = jnp.where(lane == 2 * side, mean_u[0], ends)
        ends = jnp.where(lane == 2 * side + 1, mean_v[0], ends)
    ends = jnp.concatenate([ends, jnp.zeros((LEVELS - oy, LEVELS), F32)], axis=0).T
    ex_s[0, 0:2, :] = ends[0:2]
    ex_s[1, 0:2, :] = ends[2:4]

    for copy in fourth[:2]:
        copy.start()

    inner_cols = finish_into(inner_cols, 0, RX, 8, oy - 16)
    inner_cols = finish_into(inner_cols, ox - RX, RX, 8, oy - 16)
    blank = jnp.zeros((LEVELS - oy, LEVELS), F32)
    by_row = jnp.concatenate([first_cols, inner_cols, last_cols, blank], axis=0).T
    for c in range(2):
        means[c, pl.ds(8, ox), :] = by_row[c * NL : c * NL + ox]

    for copy in fourth:
        copy.wait()
    for c in range(2):
        means[c, 7:8, :] = ex_r[0, c : c + 1, :]
        means[c, 8 + ox : 9 + ox, :] = ex_r[1, c : c + 1, :]
    for side, line, outside, spot, near in (
        (0, 7, at_south, LEVELS - 1, (0, 2)),
        (1, 0, at_north, oy, (1, 3)),
    ):
        here = lane == spot
        column = ey_r[side].T[:, line : line + 1]
        for c in range(2):
            inner = column[c * NL : c * NL + ox]
            inner = jnp.where(outside, jnp.zeros_like(inner), inner)
            means[c, pl.ds(8, ox), :] = jnp.where(here, inner, means[c, pl.ds(8, ox), :])
            for index, row, source_x in ((near[0], 7, ox - 1), (near[1], 8 + ox, 0)):
                spot_x = c * NL + source_x
                corner = ed_r[index, line : line + 1, spot_x : spot_x + 1]
                corner = jnp.where(outside, jnp.zeros_like(corner), corner)
                means[c, row : row + 1, :] = jnp.where(here, corner, means[c, row : row + 1, :])

    gathered = jnp.concatenate(
        [means[c, pl.ds(7 + a, wx, stride=RX), :] for a in range(RX + 2) for c in range(2)], axis=0
    )
    gathered = jnp.dot(
        gathered, spread, preferred_element_type=F32, precision=lax.Precision.HIGHEST
    )
    for c in range(2):
        total = jnp.zeros((wx, LEVELS), F32)
        for a in range(RX + 2):
            start = (2 * a + c) * wx
            total = total + gathered[start : start + wx] * wanted[a]
        shift = LEVELS // 2
        while shift >= wy:
            total = total + pltpu.roll(total, shift, 1)
            shift //= 2
        current_o[c] = total[:, :wy]


def store(*refs):
    sources, targets, sems = refs[:3], refs[3:6], refs[6]
    copies = [
        pltpu.make_async_copy(source, target, sems.at[i])
        for i, (source, target) in enumerate(zip(sources, targets))
    ]
    for copy in copies:
        copy.start()
    for copy in copies:
        copy.wait()


def solution(mesh):
    size_x, size_y = mesh.shape["gx"], mesh.shape["gy"]

    def step(
        spectrum,
        courant,
        source,
        wave_land,
        stokes_kernel,
        velocity,
        coriolis,
        ocean_codes,
        ocean_weights,
        wave_codes,
        wave_weights,
    ):
        wx, wy, bins = spectrum.shape
        ox, oy, levels = velocity.shape
        turn = lambda value: jnp.transpose(value, (0, 2, 1))
        operands = (
            spectrum,
            courant,
            source,
            wave_land,
            stokes_kernel,
            velocity,
            coriolis,
            turn(ocean_codes),
            turn(ocean_weights),
            turn(wave_codes),
            turn(wave_weights),
        )
        vmem = pltpu.VMEM
        edge_x = vmem((2, oy, levels), BF16)
        edge_y = vmem((2, ox, levels), BF16)
        prof_edge = vmem((2, wx, levels), BF16)
        tile = vmem((2, 8, levels), F32)
        copies = 28
        scratch = [
            vmem((wx + 2, wy, bins), BF16),
            vmem((2, bins), F32),
            vmem((wx, wy), F32),
            vmem((wx, wy), jnp.int32),
            vmem((bins, levels), BF16),
            vmem((ox + 4, oy + 16, levels), F32),
            vmem((ox + 4, oy + 16, levels), F32),
            vmem((ox, oy), F32),
            vmem((ox, K, oy), jnp.int32),
            vmem((ox, K, oy), F32),
            vmem((wx, K, wy), jnp.int32),
            vmem((wx, K, wy), F32),
            pltpu.SemaphoreType.DMA((11,)),
            vmem((4, wx, bins), F32),
            vmem((2, wx, bins), BF16),
            vmem((2, wx, bins), BF16),
            vmem((2, wx, bins), F32),
            edge_x,
            edge_x,
            edge_y,
            edge_y,
            edge_x,
            edge_x,
            edge_y,
            edge_y,
            vmem((4 * wx, bins), BF16),
            vmem((wx + 3, PITCH, levels), F32),
            prof_edge,
            prof_edge,
            prof_edge,
            prof_edge,
            prof_edge,
            vmem((4, wx, levels), BF16),
            vmem((wx, levels, 2 * levels), BF16),
            vmem((ox, oy, levels), F32),
            vmem((ox, oy, levels), F32),
            vmem((8, bins), F32),
            vmem((2, ox + 16, levels), F32),
            tile,
            tile,
            tile,
            tile,
            vmem((4, 8, levels), F32),
            pltpu.SemaphoreType.DMA((copies,)),
            pltpu.SemaphoreType.DMA((copies,)),
        ]
        body = lambda *refs: kernel(size_x, size_y, *refs)
        results = pl.pallas_call(
            body,
            out_shape=(
                pltpu.VMEM((wx, wy, bins), BF16),
                pltpu.VMEM((ox, oy, levels), F32),
                pltpu.VMEM((2, wx, wy), F32),
            ),
            in_specs=[pl.BlockSpec(memory_space=pltpu.HBM)] * len(operands),
            out_specs=(pl.BlockSpec(memory_space=pltpu.VMEM),) * 3,
            scratch_shapes=scratch,
            compiler_params=pltpu.CompilerParams(
                collective_id=0, has_side_effects=True, vmem_limit_bytes=40000000
            ),
            name="coupled_step",
        )(*[pltpu.with_memory_space_constraint(o, pltpu.HBM) for o in operands])
        return pl.pallas_call(
            store,
            out_shape=tuple(jax.ShapeDtypeStruct(r.shape, r.dtype) for r in results),
            in_specs=[pl.BlockSpec(memory_space=pltpu.VMEM)] * 3,
            out_specs=(pl.BlockSpec(memory_space=pltpu.HBM),) * 3,
            scratch_shapes=[pltpu.SemaphoreType.DMA((3,))],
            compiler_params=pltpu.CompilerParams(vmem_limit_bytes=40000000),
            name="store_results",
        )(*[pltpu.with_memory_space_constraint(r, pltpu.VMEM) for r in results])

    return jax.shard_map(
        step,
        mesh=mesh,
        in_specs=(
            P("gx", "gy", None),
            P(),
            P("gx", "gy"),
            P("gx", "gy"),
            P(),
            P("gx", "gy", None),
            P("gx", "gy"),
            P("gx", "gy", None),
            P("gx", "gy", None),
            P("gx", "gy", None),
            P("gx", "gy", None),
        ),
        out_specs=(P("gx", "gy", None), P("gx", "gy", None), P(None, "gx", "gy")),
        check_vma=False,
    )
```

```python
import jax
import jax.numpy as jnp
from jax import lax
from jax.experimental import pallas as pl
from jax.experimental.pallas import tpu as pltpu
from jax.sharding import PartitionSpec as P

NL = 64
LEVELS = 2 * NL
K = 4
RX = 2
RY = 4
PITCH = 32
MESH = pl.DeviceIdType.MESH
F32 = jnp.float32
BF16 = jnp.bfloat16

time_step = 0.5


def kernel(
    size_x,
    size_y,
    spectrum_h,
    courant_h,
    source_h,
    land_h,
    stokes_h,
    velocity_h,
    coriolis_h,
    ocodes_h,
    oweights_h,
    wcodes_h,
    wweights_h,
    spectrum_o,
    velocity_o,
    current_o,
    cells,
    courant,
    source,
    land,
    stokes_kernel,
    wide,
    middle,
    coriolis,
    ocodes,
    oweights,
    wcodes,
    wweights,
    load_sem,
    edge_f,
    edge_s,
    edge_r,
    south_north,
    vx_s,
    vx_r,
    vy_s,
    vy_r,
    mx_s,
    mx_r,
    my_s,
    my_r,
    strip,
    prof,
    px_s,
    px_r,
    py_s,
    py_r,
    pd_s,
    pd_r,
    select,
    stokes,
    cor,
    coef,
    means,
    ex_s,
    ex_r,
    ey_s,
    ey_r,
    ed_r,
    send_sem,
    recv_sem,
):
    wx, wy, bins = spectrum_o.shape
    ox, oy = velocity_o.shape[:2]
    ix, iy = lax.axis_index("gx"), lax.axis_index("gy")
    at_south, at_north = iy == 0, iy == size_y - 1

    def peer(dx, dy):
        return (lax.rem(ix + dx + size_x, size_x), lax.rem(iy + dy + size_y, size_y))

    straight = ((-1, 0), (1, 0), (0, -1), (0, 1))
    barrier = pltpu.get_barrier_semaphore()
    for step in straight:
        pl.semaphore_signal(barrier, inc=1, device_id=peer(*step), device_id_type=MESH)

    loads = [
        pltpu.make_async_copy(src, dst, load_sem.at[i])
        for i, (src, dst) in enumerate(
            (
                (spectrum_h, cells.at[pl.ds(1, wx)]),
                (velocity_h, wide.at[pl.ds(2, ox), pl.ds(8, oy)]),
                (ocodes_h, ocodes),
                (oweights_h, oweights),
                (coriolis_h, coriolis),
                (wcodes_h, wcodes),
                (wweights_h, wweights),
                (courant_h, courant),
                (source_h, source),
                (land_h, land),
                (stokes_h, stokes_kernel),
            )
        )
    ]
    for load in loads:
        load.start()

    count = [0]

    def remote(src, dst, step):
        i = count[0]
        count[0] += 1
        return pltpu.make_async_remote_copy(
            src_ref=src,
            dst_ref=dst,
            send_sem=send_sem.at[i],
            recv_sem=recv_sem.at[i],
            device_id=peer(*step),
            device_id_type=MESH,
        )

    lane = lax.broadcasted_iota(jnp.int32, (1, LEVELS), 1)
    low = lane < NL

    def swap(value):
        return pltpu.roll(value, NL, 1)

    def pack_x(ref, side, row):
        edge = jnp.where(low, swap(ref[row, pl.ds(8, oy), :]), ref[row + 1, pl.ds(8, oy), :])
        side[...] = edge.astype(BF16)

    def pack_y(ref, side, col):
        edge = jnp.where(low, ref[pl.ds(2, ox), col, :], swap(ref[pl.ds(2, ox), col + 1, :]))
        side[...] = edge.astype(BF16)

    def unpack_x(ref, side, row):
        edge = side[...].astype(F32)
        ref[row, pl.ds(8, oy), :] = swap(edge)
        ref[row + 1, pl.ds(8, oy), :] = edge

    def unpack_y(ref, side, col, outside):
        edge = side[...].astype(F32)
        edge = jnp.where(outside, jnp.zeros_like(edge), edge)
        ref[pl.ds(2, ox), col, :] = edge
        ref[pl.ds(2, ox), col + 1, :] = swap(edge)

    loads[0].wait()
    for x in range(wx):
        row = cells[x + 1].astype(F32)
        for slot, col in enumerate((0, 1, wy - 2, wy - 1)):
            edge_f[slot, x : x + 1, :] = row[col : col + 1]
    edge_s[0] = edge_f[0].astype(BF16)
    edge_s[1] = edge_f[3].astype(BF16)
    loads[1].wait()
    pack_x(wide, vx_s.at[0], 2)
    pack_x(wide, vx_s.at[1], ox)
    pack_y(wide, vy_s.at[0], 8)
    pack_y(wide, vy_s.at[1], 6 + oy)

    pl.semaphore_wait(barrier, 4)
    first = [
        remote(cells.at[wx], cells.at[0], (1, 0)),
        remote(cells.at[1], cells.at[wx + 1], (-1, 0)),
        remote(edge_s.at[1], edge_r.at[0], (0, 1)),
        remote(edge_s.at[0], edge_r.at[1], (0, -1)),
        remote(vx_s.at[1], vx_r.at[0], (1, 0)),
        remote(vx_s.at[0], vx_r.at[1], (-1, 0)),
        remote(vy_s.at[1], vy_r.at[0], (0, 1)),
        remote(vy_s.at[0], vy_r.at[1], (0, -1)),
    ]
    for copy in first[:4]:
        copy.start()

    for load in loads[2:]:
        load.wait()
    prof[...] = jnp.zeros_like(prof)
    means[...] = jnp.zeros_like(means)
    speed_x, speed_y = courant[0:1, :], courant[1:2, :]
    coef[0:1, :] = 1.0 - jnp.abs(speed_x) - jnp.abs(speed_y)
    coef[1:2, :] = jnp.maximum(speed_x, 0.0)
    coef[2:3, :] = jnp.maximum(-speed_x, 0.0)
    coef[3:4, :] = jnp.maximum(speed_y, 0.0)
    coef[4:5, :] = jnp.maximum(-speed_y, 0.0)

    slot_row = lax.broadcasted_iota(jnp.int32, (LEVELS, LEVELS), 0)
    own_cell = lax.rem(lane, oy) // RY

    def choose(i):
        def pair(ref, entry):
            return jnp.concatenate(
                [ref[RX * i, entry : entry + 1, :], ref[RX * i + 1, entry : entry + 1, :]], axis=1
            )

        weights = [pair(oweights, entry) for entry in range(K)]
        total = weights[0] + weights[1] + weights[2] + weights[3]
        rows = jnp.zeros((LEVELS, LEVELS), F32)
        for entry in range(K):
            code = pair(ocodes, entry)
            third = lax.shift_right_logical(code * 11, 5)
            slot = third * (PITCH - 3) + code + own_cell
            rows = rows + jnp.where(slot_row == slot, weights[entry] / total, 0.0)
        rows = rows.T
        high = rows.astype(BF16)
        select[i, :, 0:LEVELS] = high
        select[i, :, LEVELS : 2 * LEVELS] = (rows - high.astype(F32)).astype(BF16)

    @pl.loop(0, wx // 4)
    def _(group):
        for part in range(4):
            choose(4 * group + part)

    for copy in first[:4]:
        copy.wait()
    for side, outside in ((0, at_south), (1, at_north)):
        value = edge_r[side].astype(F32)
        south_north[side] = jnp.where(outside, jnp.zeros_like(value), value)

    growth = land[...].astype(F32)
    gain_rows = growth * (1.0 + 0.2 * source[...])
    damp_rows = 0.1 * growth
    gain, damp = gain_rows.T, damp_rows.T
    chunk = 3 * LEVELS
    cell_x = lax.broadcasted_iota(jnp.int32, (wx, chunk), 0)
    cell_y = lax.broadcasted_iota(jnp.int32, (wy, chunk), 0)

    def updated(span, center, west, east, south, north, gain_x, damp_x):
        advected = (
            coef[0:1, span] * center
            + coef[1:2, span] * west
            + coef[2:3, span] * east
            + coef[3:4, span] * south
            + coef[4:5, span] * north
        )
        return (advected * (gain_x - damp_x * advected)).astype(BF16)

    def update_row(x):
        here = lax.broadcasted_iota(jnp.int32, (wy, wx), 1) == x
        gain_x = jnp.sum(jnp.where(here, gain, 0.0), axis=1, keepdims=True)
        damp_x = jnp.sum(jnp.where(here, damp, 0.0), axis=1, keepdims=True)
        for start in range(0, bins, chunk):
            span = pl.ds(start, chunk)
            center = cells[x + 1, :, span].astype(F32)
            south = jnp.where(cell_y == 0, south_north[0, pl.ds(x, 1), span], pltpu.roll(center, 1, 0))
            north = jnp.where(
                cell_y == wy - 1, south_north[1, pl.ds(x, 1), span], pltpu.roll(center, wy - 1, 0)
            )
            west, east = cells[x, :, span].astype(F32), cells[x + 2, :, span].astype(F32)
            spectrum_o[x, :, span] = updated(span, center, west, east, south, north, gain_x, damp_x)

    def as_profile(value):
        value = jnp.dot(value, stokes_kernel[...], preferred_element_type=F32)
        value = value.astype(BF16).astype(F32)
        return jnp.where(low, swap(value), -swap(value))

    update_row(0)
    update_row(wx - 1)
    strip[0:wx] = spectrum_o[0]
    strip[wx : 2 * wx] = spectrum_o[wx - 1]
    second = [
        remote(px_s.at[1], px_r.at[0], (1, 0)),
        remote(px_s.at[0], px_r.at[1], (-1, 0)),
        remote(py_s.at[1], py_r.at[0], (0, 1)),
        remote(py_s.at[0], py_r.at[1], (0, -1)),
        remote(px_s.at[1], pd_r.at[0], (1, 1)),
        remote(px_s.at[1], pd_r.at[1], (1, -1)),
        remote(px_s.at[0], pd_r.at[2], (-1, 1)),
        remote(px_s.at[0], pd_r.at[3], (-1, -1)),
    ]
    outermost = as_profile(strip[0 : 2 * wx]).astype(BF16)
    px_s[0] = outermost[0:wx]
    px_s[1] = outermost[wx : 2 * wx]
    for copy in second[4:] + second[:2]:
        copy.start()
    for side, col in ((0, 0), (1, wy - 1)):
        for start in range(0, bins, chunk):
            span = pl.ds(start, chunk)
            center = edge_f[3 * side, :, span]
            before = cells[0, :, span].astype(F32)[col : col + 1]
            after = cells[wx + 1, :, span].astype(F32)[col : col + 1]
            west = jnp.where(cell_x == 0, before, pltpu.roll(center, 1, 0))
            east = jnp.where(cell_x == wx - 1, after, pltpu.roll(center, wx - 1, 0))
            inner, outer = edge_f[1 + side, :, span], south_north[side, :, span]
            south, north = (inner, outer) if side else (outer, inner)
            strip[(2 + side) * wx : (3 + side) * wx, span] = updated(
                span, center, west, east, south, north,
                gain_rows[:, col : col + 1], damp_rows[:, col : col + 1],
            )
    outermost = as_profile(strip[2 * wx : 4 * wx]).astype(BF16)
    py_s[0] = outermost[0:wx]
    py_s[1] = outermost[wx : 2 * wx]
    for copy in second[2:4] + first[4:]:
        copy.start()

    @pl.loop(1, wx - 1)
    def _(x):
        update_row(x)

    turned = coriolis[...].T

    @pl.loop(0, ox // 8)
    def _(group):
        for part in range(8):
            x = 8 * group + part
            here = lax.broadcasted_iota(jnp.int32, (oy, ox), 1) == x
            column = jnp.sum(jnp.where(here, turned, 0.0), axis=1, keepdims=True)
            cor[x] = jnp.broadcast_to(column, (oy, LEVELS))

    own = as_profile(spectrum_o[...].reshape(wx * wy, bins))
    prof[pl.ds(1, wx), pl.ds(1, wy), :] = own.reshape(wx, wy, LEVELS)
    for copy in first[4:]:
        copy.wait()
    unpack_x(wide, vx_r.at[0], 0)
    unpack_x(wide, vx_r.at[1], ox + 2)
    unpack_y(wide, vy_r.at[0], 6, at_south)
    unpack_y(wide, vy_r.at[1], 8 + oy, at_north)
    for copy in second:
        copy.wait()
    prof[0, pl.ds(1, wy), :] = px_r[0].astype(F32)
    prof[wx + 1, pl.ds(1, wy), :] = px_r[1].astype(F32)
    for side, outside, col in ((0, at_south, 0), (1, at_north, wy + 1)):
        value = py_r[side].astype(F32)
        prof[pl.ds(1, wx), col, :] = jnp.where(outside, jnp.zeros_like(value), value)
    for i, row, col, outside, line in (
        (0, 0, 0, at_south, wy - 1),
        (1, 0, wy + 1, at_north, 0),
        (2, wx + 1, 0, at_south, wy - 1),
        (3, wx + 1, wy + 1, at_north, 0),
    ):
        value = pd_r[i].astype(F32)[line : line + 1]
        prof[row, col : col + 1, :] = jnp.where(outside, jnp.zeros_like(value), value)

    c1 = jnp.where(low, -8.0 / 12.0, 8.0 / 12.0)
    c2 = jnp.where(low, -1.0 / 12.0, 1.0 / 12.0)

    def block(ref, x, rows, y, cols):
        return ref[pl.ds(x + 2, rows), pl.ds(y + 8, cols), :]

    def absolute(ref, x, rows, y, cols):
        def ahead(step):
            return jnp.where(
                low, block(ref, x, rows, y + step, cols), block(ref, x + step, rows, y, cols)
            )

        turn = c1 * (ahead(1) - ahead(-1)) - c2 * (ahead(2) - ahead(-2))
        return cor[pl.ds(x, rows), pl.ds(y, cols), :] + turn + pltpu.roll(turn, NL, 2)

    def advance(x, rows, y, cols):
        drift = stokes[pl.ds(x, rows), pl.ds(y, cols), :]
        middle[pl.ds(x + 2, rows), pl.ds(y + 8, cols), :] = (
            block(wide, x, rows, y, cols) + time_step * absolute(wide, x, rows, y, cols) * drift
        )

    @pl.loop(0, wx // 8)
    def _(group):
        for part in range(8):
            i = 8 * group + part
            near = prof[pl.ds(i, 4)].reshape(4 * PITCH, LEVELS).astype(BF16)
            near = jnp.concatenate([near, near], axis=0)
            both = jnp.dot(select[i], near, preferred_element_type=F32)
            stokes[pl.ds(RX * i, RX)] = both.reshape(RX, oy, LEVELS)

    advance(0, 2, 0, oy)
    advance(ox - 2, 2, 0, oy)
    pack_x(middle, mx_s.at[0], 2)
    pack_x(middle, mx_s.at[1], ox)
    third = [
        remote(mx_s.at[1], mx_r.at[0], (1, 0)),
        remote(mx_s.at[0], mx_r.at[1], (-1, 0)),
        remote(my_s.at[1], my_r.at[0], (0, 1)),
        remote(my_s.at[0], my_r.at[1], (0, -1)),
    ]
    for copy in third[:2]:
        copy.start()

    for i in range(0, ox, 8):
        advance(i, 8, 0, 8)
        advance(i, 8, oy - 8, 8)

    pack_y(middle, my_s.at[0], 8)
    pack_y(middle, my_s.at[1], 6 + oy)
    for copy in third[2:]:
        copy.start()

    @pl.loop(0, wx)
    def _(i):
        advance(RX * i, RX, 8, oy - 16)

    def finish(x, rows, y, cols):
        rate = absolute(middle, x, rows, y, cols) * stokes[pl.ds(x, rows), pl.ds(y, cols), :]
        old = block(wide, x, rows, y, cols) + block(middle, x, rows, y, cols)
        value = 0.5 * old + (0.5 * time_step) * rate
        velocity_o[pl.ds(x, rows), pl.ds(y, cols), :] = value
        mean_u = jnp.sum(jnp.where(low, value, 0.0), axis=2, keepdims=True)
        mean_v = jnp.sum(jnp.where(low, 0.0, value), axis=2, keepdims=True)
        return mean_u * (1.0 / NL), mean_v * (1.0 / NL)

    def finish_into(table, x, rows, y, cols):
        mean_u, mean_v = finish(x, rows, y, cols)
        for row in range(rows):
            table = jnp.where(lane == x + row, mean_u[row], table)
            table = jnp.where(lane == x + row + NL, mean_v[row], table)
        return table

    inner_cols = lax.fori_loop(
        1,
        wx - 1,
        lambda i, table: finish_into(table, RX * i, RX, 8, oy - 16),
        jnp.zeros((oy - 16, LEVELS), F32),
    )

    target = lax.broadcasted_iota(jnp.int32, (LEVELS, LEVELS), 1)
    origin = lax.broadcasted_iota(jnp.int32, (LEVELS, LEVELS), 0)
    offset = RY * lax.rem(target, wy) + target // wy - 1
    used = lane < (RY + 2) * wy
    spread = jnp.where((origin == (offset & (LEVELS - 1))) & used, 1.0, 0.0)
    repeat = LEVELS // wy
    wave_sum = wweights[:, 0, :] + wweights[:, 1, :] + wweights[:, 2, :] + wweights[:, 3, :]
    tiled = [
        (
            jnp.concatenate([wcodes[:, entry, :]] * repeat, axis=1),
            jnp.concatenate([wweights[:, entry, :] / wave_sum] * repeat, axis=1),
        )
        for entry in range(K)
    ]
    wanted = []
    for a in range(RX + 2):
        number = (RY + 2) * a + lane // wy
        chosen = jnp.zeros((wx, LEVELS), F32)
        for code, weight in tiled:
            chosen = chosen + jnp.where((code == number) & used, weight, 0.0)
        wanted.append(chosen)

    for copy in third:
        copy.wait()
    unpack_x(middle, mx_r.at[0], 0)
    unpack_x(middle, mx_r.at[1], ox + 2)
    unpack_y(middle, my_r.at[0], 6, at_south)
    unpack_y(middle, my_r.at[1], 8 + oy, at_north)

    first_cols = last_cols = jnp.zeros((8, LEVELS), F32)
    for i in range(0, ox, 8):
        first_cols = finish_into(first_cols, i, 8, 0, 8)
        last_cols = finish_into(last_cols, i, 8, oy - 8, 8)
    ey_s[0] = first_cols
    ey_s[1] = last_cols
    fourth = [
        remote(ex_s.at[1], ex_r.at[0], (1, 0)),
        remote(ex_s.at[0], ex_r.at[1], (-1, 0)),
        remote(ey_s.at[1], ey_r.at[0], (0, 1)),
        remote(ey_s.at[0], ey_r.at[1], (0, -1)),
        remote(ey_s.at[1], ed_r.at[0], (1, 1)),
        remote(ey_s.at[0], ed_r.at[1], (1, -1)),
        remote(ey_s.at[1], ed_r.at[2], (-1, 1)),
        remote(ey_s.at[0], ed_r.at[3], (-1, -1)),
    ]
    for copy in fourth[4:] + fourth[2:4]:
        copy.start()
    ends = jnp.zeros((oy, LEVELS), F32)
    for side, x in ((0, 0), (1, ox - 1)):
        mean_u, mean_v = finish(x, 1, 0, oy)
        ends = jnp.where(lane == 2 * side, mean_u[0], ends)
        ends = jnp.where(lane == 2 * side + 1, mean_v[0], ends)
    ends = jnp.concatenate([ends, jnp.zeros((LEVELS - oy, LEVELS), F32)], axis=0).T
    ex_s[0, 0:2, :] = ends[0:2]
    ex_s[1, 0:2, :] = ends[2:4]

    for copy in fourth[:2]:
        copy.start()

    inner_cols = finish_into(inner_cols, 0, RX, 8, oy - 16)
    inner_cols = finish_into(inner_cols, ox - RX, RX, 8, oy - 16)
    blank = jnp.zeros((LEVELS - oy, LEVELS), F32)
    by_row = jnp.concatenate([first_cols, inner_cols, last_cols, blank], axis=0).T
    for c in range(2):
        means[c, pl.ds(8, ox), :] = by_row[c * NL : c * NL + ox]

    for copy in fourth:
        copy.wait()
    for c in range(2):
        means[c, 7:8, :] = ex_r[0, c : c + 1, :]
        means[c, 8 + ox : 9 + ox, :] = ex_r[1, c : c + 1, :]
    for side, line, outside, spot, near in (
        (0, 7, at_south, LEVELS - 1, (0, 2)),
        (1, 0, at_north, oy, (1, 3)),
    ):
        here = lane == spot
        column = ey_r[side].T[:, line : line + 1]
        for c in range(2):
            inner = column[c * NL : c * NL + ox]
            inner = jnp.where(outside, jnp.zeros_like(inner), inner)
            means[c, pl.ds(8, ox), :] = jnp.where(here, inner, means[c, pl.ds(8, ox), :])
            for index, row, source_x in ((near[0], 7, ox - 1), (near[1], 8 + ox, 0)):
                spot_x = c * NL + source_x
                corner = ed_r[index, line : line + 1, spot_x : spot_x + 1]
                corner = jnp.where(outside, jnp.zeros_like(corner), corner)
                means[c, row : row + 1, :] = jnp.where(here, corner, means[c, row : row + 1, :])

    gathered = jnp.concatenate(
        [means[c, pl.ds(7 + a, wx, stride=RX), :] for a in range(RX + 2) for c in range(2)], axis=0
    )
    gathered = jnp.dot(
        gathered, spread, preferred_element_type=F32, precision=lax.Precision.HIGHEST
    )
    for c in range(2):
        total = jnp.zeros((wx, LEVELS), F32)
        for a in range(RX + 2):
            start = (2 * a + c) * wx
            total = total + gathered[start : start + wx] * wanted[a]
        shift = LEVELS // 2
        while shift >= wy:
            total = total + pltpu.roll(total, shift, 1)
            shift //= 2
        current_o[c] = total[:, :wy]


def store(*refs):
    sources, targets, sems = refs[:3], refs[3:6], refs[6]
    copies = [
        pltpu.make_async_copy(source, target, sems.at[i])
        for i, (source, target) in enumerate(zip(sources, targets))
    ]
    for copy in copies:
        copy.start()
    for copy in copies:
        copy.wait()


def solution(mesh):
    size_x, size_y = mesh.shape["gx"], mesh.shape["gy"]

    def step(
        spectrum,
        courant,
        source,
        wave_land,
        stokes_kernel,
        velocity,
        coriolis,
        ocean_codes,
        ocean_weights,
        wave_codes,
        wave_weights,
    ):
        wx, wy, bins = spectrum.shape
        ox, oy, levels = velocity.shape
        turn = lambda value: jnp.transpose(value, (0, 2, 1))
        operands = (
            spectrum,
            courant,
            source,
            wave_land,
            stokes_kernel,
            velocity,
            coriolis,
            turn(ocean_codes),
            turn(ocean_weights),
            turn(wave_codes),
            turn(wave_weights),
        )
        vmem = pltpu.VMEM
        edge_x = vmem((2, oy, levels), BF16)
        edge_y = vmem((2, ox, levels), BF16)
        prof_edge = vmem((2, wx, levels), BF16)
        tile = vmem((2, 8, levels), F32)
        copies = 28
        scratch = [
            vmem((wx + 2, wy, bins), BF16),
            vmem((2, bins), F32),
            vmem((wx, wy), F32),
            vmem((wx, wy), jnp.int32),
            vmem((bins, levels), BF16),
            vmem((ox + 4, oy + 16, levels), F32),
            vmem((ox + 4, oy + 16, levels), F32),
            vmem((ox, oy), F32),
            vmem((ox, K, oy), jnp.int32),
            vmem((ox, K, oy), F32),
            vmem((wx, K, wy), jnp.int32),
            vmem((wx, K, wy), F32),
            pltpu.SemaphoreType.DMA((11,)),
            vmem((4, wx, bins), F32),
            vmem((2, wx, bins), BF16),
            vmem((2, wx, bins), BF16),
            vmem((2, wx, bins), F32),
            edge_x,
            edge_x,
            edge_y,
            edge_y,
            edge_x,
            edge_x,
            edge_y,
            edge_y,
            vmem((4 * wx, bins), BF16),
            vmem((wx + 3, PITCH, levels), F32),
            prof_edge,
            prof_edge,
            prof_edge,
            prof_edge,
            prof_edge,
            vmem((4, wx, levels), BF16),
            vmem((wx, levels, 2 * levels), BF16),
            vmem((ox, oy, levels), F32),
            vmem((ox, oy, levels), F32),
            vmem((8, bins), F32),
            vmem((2, ox + 16, levels), F32),
            tile,
            tile,
            tile,
            tile,
            vmem((4, 8, levels), F32),
            pltpu.SemaphoreType.DMA((copies,)),
            pltpu.SemaphoreType.DMA((copies,)),
        ]
        body = lambda *refs: kernel(size_x, size_y, *refs)
        results = pl.pallas_call(
            body,
            out_shape=(
                pltpu.VMEM((wx, wy, bins), BF16),
                pltpu.VMEM((ox, oy, levels), F32),
                pltpu.VMEM((2, wx, wy), F32),
            ),
            in_specs=[pl.BlockSpec(memory_space=pltpu.HBM)] * len(operands),
            out_specs=(pl.BlockSpec(memory_space=pltpu.VMEM),) * 3,
            scratch_shapes=scratch,
            compiler_params=pltpu.CompilerParams(
                collective_id=0, has_side_effects=True, vmem_limit_bytes=40000000
            ),
            name="coupled_step",
        )(*[pltpu.with_memory_space_constraint(o, pltpu.HBM) for o in operands])
        return pl.pallas_call(
            store,
            out_shape=tuple(jax.ShapeDtypeStruct(r.shape, r.dtype) for r in results),
            in_specs=[pl.BlockSpec(memory_space=pltpu.VMEM)] * 3,
            out_specs=(pl.BlockSpec(memory_space=pltpu.HBM),) * 3,
            scratch_shapes=[pltpu.SemaphoreType.DMA((3,))],
            compiler_params=pltpu.CompilerParams(vmem_limit_bytes=40000000),
            name="store_results",
        )(*[pltpu.with_memory_space_constraint(r, pltpu.VMEM) for r in results])

    return jax.shard_map(
        step,
        mesh=mesh,
        in_specs=(
            P("gx", "gy", None),
            P(),
            P("gx", "gy"),
            P("gx", "gy"),
            P(),
            P("gx", "gy", None),
            P("gx", "gy"),
            P("gx", "gy", None),
            P("gx", "gy", None),
            P("gx", "gy", None),
            P("gx", "gy", None),
        ),
        out_specs=(P("gx", "gy", None), P("gx", "gy", None), P(None, "gx", "gy")),
        check_vma=False,
    )
```

```python
import jax
import jax.numpy as jnp
from jax import lax
from jax.experimental import pallas as pl
from jax.experimental.pallas import tpu as pltpu
from jax.sharding import PartitionSpec as P

NL = 64
LEVELS = 2 * NL
K = 4
RX = 2
RY = 4
PITCH = 32
MESH = pl.DeviceIdType.MESH
F32 = jnp.float32
BF16 = jnp.bfloat16

time_step = 0.5


def kernel(
    size_x,
    size_y,
    spectrum_h,
    courant_h,
    source_h,
    land_h,
    stokes_h,
    velocity_h,
    coriolis_h,
    ocodes_h,
    oweights_h,
    wcodes_h,
    wweights_h,
    spectrum_o,
    velocity_o,
    current_o,
    cells,
    courant,
    source,
    land,
    stokes_kernel,
    wide,
    middle,
    coriolis,
    ocodes,
    oweights,
    wcodes,
    wweights,
    load_sem,
    edge_f,
    edge_s,
    edge_r,
    south_north,
    vx_s,
    vx_r,
    vy_s,
    vy_r,
    mx_s,
    mx_r,
    my_s,
    my_r,
    strip,
    prof,
    px_s,
    px_r,
    py_s,
    py_r,
    pd_s,
    pd_r,
    select,
    stokes,
    cor,
    coef,
    means,
    ex_s,
    ex_r,
    ey_s,
    ey_r,
    ed_r,
    send_sem,
    recv_sem,
):
    wx, wy, bins = spectrum_o.shape
    ox, oy = velocity_o.shape[:2]
    ix, iy = lax.axis_index("gx"), lax.axis_index("gy")
    at_south, at_north = iy == 0, iy == size_y - 1

    def peer(dx, dy):
        return (lax.rem(ix + dx + size_x, size_x), lax.rem(iy + dy + size_y, size_y))

    straight = ((-1, 0), (1, 0), (0, -1), (0, 1))
    barrier = pltpu.get_barrier_semaphore()
    for step in straight:
        pl.semaphore_signal(barrier, inc=1, device_id=peer(*step), device_id_type=MESH)

    loads = [
        pltpu.make_async_copy(src, dst, load_sem.at[i])
        for i, (src, dst) in enumerate(
            (
                (spectrum_h, cells.at[pl.ds(1, wx)]),
                (velocity_h, wide.at[pl.ds(2, ox), pl.ds(8, oy)]),
                (ocodes_h, ocodes),
                (oweights_h, oweights),
                (coriolis_h, coriolis),
                (wcodes_h, wcodes),
                (wweights_h, wweights),
                (courant_h, courant),
                (source_h, source),
                (land_h, land),
                (stokes_h, stokes_kernel),
            )
        )
    ]
    for load in loads:
        load.start()

    count = [0]

    def remote(src, dst, step):
        i = count[0]
        count[0] += 1
        return pltpu.make_async_remote_copy(
            src_ref=src,
            dst_ref=dst,
            send_sem=send_sem.at[i],
            recv_sem=recv_sem.at[i],
            device_id=peer(*step),
            device_id_type=MESH,
        )

    lane = lax.broadcasted_iota(jnp.int32, (1, LEVELS), 1)
    low = lane < NL

    def swap(value):
        return pltpu.roll(value, NL, 1)

    def pack_x(ref, side, row):
        edge = jnp.where(low, swap(ref[row, pl.ds(8, oy), :]), ref[row + 1, pl.ds(8, oy), :])
        side[...] = edge.astype(BF16)

    def pack_y(ref, side, col):
        edge = jnp.where(low, ref[pl.ds(2, ox), col, :], swap(ref[pl.ds(2, ox), col + 1, :]))
        side[...] = edge.astype(BF16)

    def unpack_x(ref, side, row):
        edge = side[...].astype(F32)
        ref[row, pl.ds(8, oy), :] = swap(edge)
        ref[row + 1, pl.ds(8, oy), :] = edge

    def unpack_y(ref, side, col, outside):
        edge = side[...].astype(F32)
        edge = jnp.where(outside, jnp.zeros_like(edge), edge)
        ref[pl.ds(2, ox), col, :] = edge
        ref[pl.ds(2, ox), col + 1, :] = swap(edge)

    loads[0].wait()
    for x in range(wx):
        row = cells[x + 1].astype(F32)
        for slot, col in enumerate((0, 1, wy - 2, wy - 1)):
            edge_f[slot, x : x + 1, :] = row[col : col + 1]
    edge_s[0] = edge_f[0].astype(BF16)
    edge_s[1] = edge_f[3].astype(BF16)
    loads[1].wait()
    pack_x(wide, vx_s.at[0], 2)
    pack_x(wide, vx_s.at[1], ox)
    pack_y(wide, vy_s.at[0], 8)
    pack_y(wide, vy_s.at[1], 6 + oy)

    pl.semaphore_wait(barrier, 4)
    first = [
        remote(cells.at[wx], cells.at[0], (1, 0)),
        remote(cells.at[1], cells.at[wx + 1], (-1, 0)),
        remote(edge_s.at[1], edge_r.at[0], (0, 1)),
        remote(edge_s.at[0], edge_r.at[1], (0, -1)),
        remote(vx_s.at[1], vx_r.at[0], (1, 0)),
        remote(vx_s.at[0], vx_r.at[1], (-1, 0)),
        remote(vy_s.at[1], vy_r.at[0], (0, 1)),
        remote(vy_s.at[0], vy_r.at[1], (0, -1)),
    ]
    for copy in first[:4]:
        copy.start()

    for load in loads[2:]:
        load.wait()
    prof[...] = jnp.zeros_like(prof)
    means[...] = jnp.zeros_like(means)
    speed_x, speed_y = courant[0:1, :], courant[1:2, :]
    coef[0:1, :] = 1.0 - jnp.abs(speed_x) - jnp.abs(speed_y)
    coef[1:2, :] = jnp.maximum(speed_x, 0.0)
    coef[2:3, :] = jnp.maximum(-speed_x, 0.0)
    coef[3:4, :] = jnp.maximum(speed_y, 0.0)
    coef[4:5, :] = jnp.maximum(-speed_y, 0.0)

    slot_row = lax.broadcasted_iota(jnp.int32, (LEVELS, LEVELS), 0)
    own_cell = lax.rem(lane, oy) // RY

    def choose(i):
        def pair(ref, entry):
            return jnp.concatenate(
                [ref[RX * i, entry : entry + 1, :], ref[RX * i + 1, entry : entry + 1, :]], axis=1
            )

        weights = [pair(oweights, entry) for entry in range(K)]
        total = weights[0] + weights[1] + weights[2] + weights[3]
        rows = jnp.zeros((LEVELS, LEVELS), F32)
        for entry in range(K):
            code = pair(ocodes, entry)
            third = lax.shift_right_logical(code * 11, 5)
            slot = third * (PITCH - 3) + code + own_cell
            rows = rows + jnp.where(slot_row == slot, weights[entry] / total, 0.0)
        rows = rows.T
        high = rows.astype(BF16)
        select[i, :, 0:LEVELS] = high
        select[i, :, LEVELS : 2 * LEVELS] = (rows - high.astype(F32)).astype(BF16)

    @pl.loop(0, wx // 4)
    def _(group):
        for part in range(4):
            choose(4 * group + part)

    growth = land[...].astype(F32)
    gain_rows = growth * (1.0 + 0.2 * source[...])
    damp_rows = 0.1 * growth
    gain, damp = gain_rows.T, damp_rows.T
    for copy in first[:4]:
        copy.wait()
    for side, outside in ((0, at_south), (1, at_north)):
        value = edge_r[side].astype(F32)
        south_north[side] = jnp.where(outside, jnp.zeros_like(value), value)

    chunk = 3 * LEVELS
    cell_x = lax.broadcasted_iota(jnp.int32, (wx, chunk), 0)
    cell_y = lax.broadcasted_iota(jnp.int32, (wy, chunk), 0)

    def updated(span, center, west, east, south, north, gain_x, damp_x):
        advected = (
            coef[0:1, span] * center
            + coef[1:2, span] * west
            + coef[2:3, span] * east
            + coef[3:4, span] * south
            + coef[4:5, span] * north
        )
        return (advected * (gain_x - damp_x * advected)).astype(BF16)

    def update_row(x):
        here = lax.broadcasted_iota(jnp.int32, (wy, wx), 1) == x
        gain_x = jnp.sum(jnp.where(here, gain, 0.0), axis=1, keepdims=True)
        damp_x = jnp.sum(jnp.where(here, damp, 0.0), axis=1, keepdims=True)
        for start in range(0, bins, chunk):
            span = pl.ds(start, chunk)
            center = cells[x + 1, :, span].astype(F32)
            south = jnp.where(cell_y == 0, south_north[0, pl.ds(x, 1), span], pltpu.roll(center, 1, 0))
            north = jnp.where(
                cell_y == wy - 1, south_north[1, pl.ds(x, 1), span], pltpu.roll(center, wy - 1, 0)
            )
            west, east = cells[x, :, span].astype(F32), cells[x + 2, :, span].astype(F32)
            spectrum_o[x, :, span] = updated(span, center, west, east, south, north, gain_x, damp_x)

    def as_profile(value):
        value = jnp.dot(value, stokes_kernel[...], preferred_element_type=F32)
        value = value.astype(BF16).astype(F32)
        return jnp.where(low, swap(value), -swap(value))

    update_row(0)
    update_row(wx - 1)
    strip[0:wx] = spectrum_o[0]
    strip[wx : 2 * wx] = spectrum_o[wx - 1]
    second = [
        remote(px_s.at[1], px_r.at[0], (1, 0)),
        remote(px_s.at[0], px_r.at[1], (-1, 0)),
        remote(py_s.at[1], py_r.at[0], (0, 1)),
        remote(py_s.at[0], py_r.at[1], (0, -1)),
        remote(px_s.at[1], pd_r.at[0], (1, 1)),
        remote(px_s.at[1], pd_r.at[1], (1, -1)),
        remote(px_s.at[0], pd_r.at[2], (-1, 1)),
        remote(px_s.at[0], pd_r.at[3], (-1, -1)),
    ]
    outermost = as_profile(strip[0 : 2 * wx]).astype(BF16)
    px_s[0] = outermost[0:wx]
    px_s[1] = outermost[wx : 2 * wx]
    for copy in second[4:] + second[:2]:
        copy.start()
    for side, col in ((0, 0), (1, wy - 1)):
        for start in range(0, bins, chunk):
            span = pl.ds(start, chunk)
            center = edge_f[3 * side, :, span]
            before = cells[0, :, span].astype(F32)[col : col + 1]
            after = cells[wx + 1, :, span].astype(F32)[col : col + 1]
            west = jnp.where(cell_x == 0, before, pltpu.roll(center, 1, 0))
            east = jnp.where(cell_x == wx - 1, after, pltpu.roll(center, wx - 1, 0))
            inner, outer = edge_f[1 + side, :, span], south_north[side, :, span]
            south, north = (inner, outer) if side else (outer, inner)
            strip[(2 + side) * wx : (3 + side) * wx, span] = updated(
                span, center, west, east, south, north,
                gain_rows[:, col : col + 1], damp_rows[:, col : col + 1],
            )
    outermost = as_profile(strip[2 * wx : 4 * wx]).astype(BF16)
    py_s[0] = outermost[0:wx]
    py_s[1] = outermost[wx : 2 * wx]
    for copy in second[2:4] + first[4:]:
        copy.start()

    @pl.loop(1, wx - 1)
    def _(x):
        update_row(x)

    turned = coriolis[...].T

    @pl.loop(0, ox // 8)
    def _(group):
        for part in range(8):
            x = 8 * group + part
            here = lax.broadcasted_iota(jnp.int32, (oy, ox), 1) == x
            column = jnp.sum(jnp.where(here, turned, 0.0), axis=1, keepdims=True)
            cor[x] = jnp.broadcast_to(column, (oy, LEVELS))

    own = as_profile(spectrum_o[...].reshape(wx * wy, bins))
    prof[pl.ds(1, wx), pl.ds(1, wy), :] = own.reshape(wx, wy, LEVELS)
    for copy in first[4:]:
        copy.wait()
    unpack_x(wide, vx_r.at[0], 0)
    unpack_x(wide, vx_r.at[1], ox + 2)
    unpack_y(wide, vy_r.at[0], 6, at_south)
    unpack_y(wide, vy_r.at[1], 8 + oy, at_north)
    for copy in second:
        copy.wait()
    prof[0, pl.ds(1, wy), :] = px_r[0].astype(F32)
    prof[wx + 1, pl.ds(1, wy), :] = px_r[1].astype(F32)
    for side, outside, col in ((0, at_south, 0), (1, at_north, wy + 1)):
        value = py_r[side].astype(F32)
        prof[pl.ds(1, wx), col, :] = jnp.where(outside, jnp.zeros_like(value), value)
    for i, row, col, outside, line in (
        (0, 0, 0, at_south, wy - 1),
        (1, 0, wy + 1, at_north, 0),
        (2, wx + 1, 0, at_south, wy - 1),
        (3, wx + 1, wy + 1, at_north, 0),
    ):
        value = pd_r[i].astype(F32)[line : line + 1]
        prof[row, col : col + 1, :] = jnp.where(outside, jnp.zeros_like(value), value)

    c1 = jnp.where(low, -8.0 / 12.0, 8.0 / 12.0)
    c2 = jnp.where(low, -1.0 / 12.0, 1.0 / 12.0)

    def block(ref, x, rows, y, cols):
        return ref[pl.ds(x + 2, rows), pl.ds(y + 8, cols), :]

    def absolute(ref, x, rows, y, cols):
        def ahead(step):
            return jnp.where(
                low, block(ref, x, rows, y + step, cols), block(ref, x + step, rows, y, cols)
            )

        turn = c1 * (ahead(1) - ahead(-1)) - c2 * (ahead(2) - ahead(-2))
        return cor[pl.ds(x, rows), pl.ds(y, cols), :] + turn + pltpu.roll(turn, NL, 2)

    def advance(x, rows, y, cols):
        drift = stokes[pl.ds(x, rows), pl.ds(y, cols), :]
        middle[pl.ds(x + 2, rows), pl.ds(y + 8, cols), :] = (
            block(wide, x, rows, y, cols) + time_step * absolute(wide, x, rows, y, cols) * drift
        )

    def drift_row(i):
        near = prof[pl.ds(i, 4)].reshape(4 * PITCH, LEVELS).astype(BF16)
        near = jnp.concatenate([near, near], axis=0)
        both = jnp.dot(select[i], near, preferred_element_type=F32)
        stokes[pl.ds(RX * i, RX)] = both.reshape(RX, oy, LEVELS)

    drift_row(0)
    drift_row(wx - 1)
    advance(0, 2, 0, oy)
    advance(ox - 2, 2, 0, oy)
    pack_x(middle, mx_s.at[0], 2)
    pack_x(middle, mx_s.at[1], ox)
    third = [
        remote(mx_s.at[1], mx_r.at[0], (1, 0)),
        remote(mx_s.at[0], mx_r.at[1], (-1, 0)),
        remote(my_s.at[1], my_r.at[0], (0, 1)),
        remote(my_s.at[0], my_r.at[1], (0, -1)),
    ]
    for copy in third[:2]:
        copy.start()

    for i in range(1, wx - 1):
        drift_row(i)
    for i in range(0, ox, 8):
        advance(i, 8, 0, 8)
        advance(i, 8, oy - 8, 8)

    pack_y(middle, my_s.at[0], 8)
    pack_y(middle, my_s.at[1], 6 + oy)
    for copy in third[2:]:
        copy.start()

    @pl.loop(0, wx)
    def _(i):
        advance(RX * i, RX, 8, oy - 16)

    def finish(x, rows, y, cols):
        rate = absolute(middle, x, rows, y, cols) * stokes[pl.ds(x, rows), pl.ds(y, cols), :]
        old = block(wide, x, rows, y, cols) + block(middle, x, rows, y, cols)
        value = 0.5 * old + (0.5 * time_step) * rate
        velocity_o[pl.ds(x, rows), pl.ds(y, cols), :] = value
        mean_u = jnp.sum(jnp.where(low, value, 0.0), axis=2, keepdims=True)
        mean_v = jnp.sum(jnp.where(low, 0.0, value), axis=2, keepdims=True)
        return mean_u * (1.0 / NL), mean_v * (1.0 / NL)

    def finish_into(table, x, rows, y, cols):
        mean_u, mean_v = finish(x, rows, y, cols)
        for row in range(rows):
            table = jnp.where(lane == x + row, mean_u[row], table)
            table = jnp.where(lane == x + row + NL, mean_v[row], table)
        return table

    inner_cols = lax.fori_loop(
        1,
        wx - 1,
        lambda i, table: finish_into(table, RX * i, RX, 8, oy - 16),
        jnp.zeros((oy - 16, LEVELS), F32),
    )

    target = lax.broadcasted_iota(jnp.int32, (LEVELS, LEVELS), 1)
    origin = lax.broadcasted_iota(jnp.int32, (LEVELS, LEVELS), 0)
    offset = RY * lax.rem(target, wy) + target // wy - 1
    used = lane < (RY + 2) * wy
    spread = jnp.where((origin == (offset & (LEVELS - 1))) & used, 1.0, 0.0)
    repeat = LEVELS // wy
    wave_sum = wweights[:, 0, :] + wweights[:, 1, :] + wweights[:, 2, :] + wweights[:, 3, :]
    tiled = [
        (
            jnp.concatenate([wcodes[:, entry, :]] * repeat, axis=1),
            jnp.concatenate([wweights[:, entry, :] / wave_sum] * repeat, axis=1),
        )
        for entry in range(K)
    ]
    wanted = []
    for a in range(RX + 2):
        number = (RY + 2) * a + lane // wy
        chosen = jnp.zeros((wx, LEVELS), F32)
        for code, weight in tiled:
            chosen = chosen + jnp.where((code == number) & used, weight, 0.0)
        wanted.append(chosen)

    for copy in third:
        copy.wait()
    unpack_x(middle, mx_r.at[0], 0)
    unpack_x(middle, mx_r.at[1], ox + 2)
    unpack_y(middle, my_r.at[0], 6, at_south)
    unpack_y(middle, my_r.at[1], 8 + oy, at_north)

    first_cols = last_cols = jnp.zeros((8, LEVELS), F32)
    for i in range(0, ox, 8):
        first_cols = finish_into(first_cols, i, 8, 0, 8)
        last_cols = finish_into(last_cols, i, 8, oy - 8, 8)
    ey_s[0] = first_cols
    ey_s[1] = last_cols
    fourth = [
        remote(ex_s.at[1], ex_r.at[0], (1, 0)),
        remote(ex_s.at[0], ex_r.at[1], (-1, 0)),
        remote(ey_s.at[1], ey_r.at[0], (0, 1)),
        remote(ey_s.at[0], ey_r.at[1], (0, -1)),
        remote(ey_s.at[1], ed_r.at[0], (1, 1)),
        remote(ey_s.at[0], ed_r.at[1], (1, -1)),
        remote(ey_s.at[1], ed_r.at[2], (-1, 1)),
        remote(ey_s.at[0], ed_r.at[3], (-1, -1)),
    ]
    for copy in fourth[4:] + fourth[2:4]:
        copy.start()
    ends = jnp.zeros((oy, LEVELS), F32)
    for side, x in ((0, 0), (1, ox - 1)):
        mean_u, mean_v = finish(x, 1, 0, oy)
        ends = jnp.where(lane == 2 * side, mean_u[0], ends)
        ends = jnp.where(lane == 2 * side + 1, mean_v[0], ends)
    ends = jnp.concatenate([ends, jnp.zeros((LEVELS - oy, LEVELS), F32)], axis=0).T
    ex_s[0, 0:2, :] = ends[0:2]
    ex_s[1, 0:2, :] = ends[2:4]

    for copy in fourth[:2]:
        copy.start()

    inner_cols = finish_into(inner_cols, 0, RX, 8, oy - 16)
    inner_cols = finish_into(inner_cols, ox - RX, RX, 8, oy - 16)
    blank = jnp.zeros((LEVELS - oy, LEVELS), F32)
    by_row = jnp.concatenate([first_cols, inner_cols, last_cols, blank], axis=0).T
    for c in range(2):
        means[c, pl.ds(8, ox), :] = by_row[c * NL : c * NL + ox]

    for copy in fourth:
        copy.wait()
    for c in range(2):
        means[c, 7:8, :] = ex_r[0, c : c + 1, :]
        means[c, 8 + ox : 9 + ox, :] = ex_r[1, c : c + 1, :]
    for side, line, outside, spot, near in (
        (0, 7, at_south, LEVELS - 1, (0, 2)),
        (1, 0, at_north, oy, (1, 3)),
    ):
        here = lane == spot
        column = ey_r[side].T[:, line : line + 1]
        for c in range(2):
            inner = column[c * NL : c * NL + ox]
            inner = jnp.where(outside, jnp.zeros_like(inner), inner)
            means[c, pl.ds(8, ox), :] = jnp.where(here, inner, means[c, pl.ds(8, ox), :])
            for index, row, source_x in ((near[0], 7, ox - 1), (near[1], 8 + ox, 0)):
                spot_x = c * NL + source_x
                corner = ed_r[index, line : line + 1, spot_x : spot_x + 1]
                corner = jnp.where(outside, jnp.zeros_like(corner), corner)
                means[c, row : row + 1, :] = jnp.where(here, corner, means[c, row : row + 1, :])

    gathered = jnp.concatenate(
        [means[c, pl.ds(7 + a, wx, stride=RX), :] for a in range(RX + 2) for c in range(2)], axis=0
    )
    gathered = jnp.dot(
        gathered, spread, preferred_element_type=F32, precision=lax.Precision.HIGHEST
    )
    for c in range(2):
        total = jnp.zeros((wx, LEVELS), F32)
        for a in range(RX + 2):
            start = (2 * a + c) * wx
            total = total + gathered[start : start + wx] * wanted[a]
        shift = LEVELS // 2
        while shift >= wy:
            total = total + pltpu.roll(total, shift, 1)
            shift //= 2
        current_o[c] = total[:, :wy]


def store(*refs):
    sources, targets, sems = refs[:3], refs[3:6], refs[6]
    copies = [
        pltpu.make_async_copy(source, target, sems.at[i])
        for i, (source, target) in enumerate(zip(sources, targets))
    ]
    for copy in copies:
        copy.start()
    for copy in copies:
        copy.wait()


def solution(mesh):
    size_x, size_y = mesh.shape["gx"], mesh.shape["gy"]

    def step(
        spectrum,
        courant,
        source,
        wave_land,
        stokes_kernel,
        velocity,
        coriolis,
        ocean_codes,
        ocean_weights,
        wave_codes,
        wave_weights,
    ):
        wx, wy, bins = spectrum.shape
        ox, oy, levels = velocity.shape
        turn = lambda value: jnp.transpose(value, (0, 2, 1))
        operands = (
            spectrum,
            courant,
            source,
            wave_land,
            stokes_kernel,
            velocity,
            coriolis,
            turn(ocean_codes),
            turn(ocean_weights),
            turn(wave_codes),
            turn(wave_weights),
        )
        vmem = pltpu.VMEM
        edge_x = vmem((2, oy, levels), BF16)
        edge_y = vmem((2, ox, levels), BF16)
        prof_edge = vmem((2, wx, levels), BF16)
        tile = vmem((2, 8, levels), F32)
        copies = 28
        scratch = [
            vmem((wx + 2, wy, bins), BF16),
            vmem((2, bins), F32),
            vmem((wx, wy), F32),
            vmem((wx, wy), jnp.int32),
            vmem((bins, levels), BF16),
            vmem((ox + 4, oy + 16, levels), F32),
            vmem((ox + 4, oy + 16, levels), F32),
            vmem((ox, oy), F32),
            vmem((ox, K, oy), jnp.int32),
            vmem((ox, K, oy), F32),
            vmem((wx, K, wy), jnp.int32),
            vmem((wx, K, wy), F32),
            pltpu.SemaphoreType.DMA((11,)),
            vmem((4, wx, bins), F32),
            vmem((2, wx, bins), BF16),
            vmem((2, wx, bins), BF16),
            vmem((2, wx, bins), F32),
            edge_x,
            edge_x,
            edge_y,
            edge_y,
            edge_x,
            edge_x,
            edge_y,
            edge_y,
            vmem((4 * wx, bins), BF16),
            vmem((wx + 3, PITCH, levels), F32),
            prof_edge,
            prof_edge,
            prof_edge,
            prof_edge,
            prof_edge,
            vmem((4, wx, levels), BF16),
            vmem((wx, levels, 2 * levels), BF16),
            vmem((ox, oy, levels), F32),
            vmem((ox, oy, levels), F32),
            vmem((8, bins), F32),
            vmem((2, ox + 16, levels), F32),
            tile,
            tile,
            tile,
            tile,
            vmem((4, 8, levels), F32),
            pltpu.SemaphoreType.DMA((copies,)),
            pltpu.SemaphoreType.DMA((copies,)),
        ]
        body = lambda *refs: kernel(size_x, size_y, *refs)
        results = pl.pallas_call(
            body,
            out_shape=(
                pltpu.VMEM((wx, wy, bins), BF16),
                pltpu.VMEM((ox, oy, levels), F32),
                pltpu.VMEM((2, wx, wy), F32),
            ),
            in_specs=[pl.BlockSpec(memory_space=pltpu.HBM)] * len(operands),
            out_specs=(pl.BlockSpec(memory_space=pltpu.VMEM),) * 3,
            scratch_shapes=scratch,
            compiler_params=pltpu.CompilerParams(
                collective_id=0, has_side_effects=True, vmem_limit_bytes=40000000
            ),
            name="coupled_step",
        )(*[pltpu.with_memory_space_constraint(o, pltpu.HBM) for o in operands])
        return pl.pallas_call(
            store,
            out_shape=tuple(jax.ShapeDtypeStruct(r.shape, r.dtype) for r in results),
            in_specs=[pl.BlockSpec(memory_space=pltpu.VMEM)] * 3,
            out_specs=(pl.BlockSpec(memory_space=pltpu.HBM),) * 3,
            scratch_shapes=[pltpu.SemaphoreType.DMA((3,))],
            compiler_params=pltpu.CompilerParams(vmem_limit_bytes=40000000),
            name="store_results",
        )(*[pltpu.with_memory_space_constraint(r, pltpu.VMEM) for r in results])

    return jax.shard_map(
        step,
        mesh=mesh,
        in_specs=(
            P("gx", "gy", None),
            P(),
            P("gx", "gy"),
            P("gx", "gy"),
            P(),
            P("gx", "gy", None),
            P("gx", "gy"),
            P("gx", "gy", None),
            P("gx", "gy", None),
            P("gx", "gy", None),
            P("gx", "gy", None),
        ),
        out_specs=(P("gx", "gy", None), P("gx", "gy", None), P(None, "gx", "gy")),
        check_vma=False,
    )
```

```python
import jax
import jax.numpy as jnp
from jax import lax
from jax.experimental import pallas as pl
from jax.experimental.pallas import tpu as pltpu
from jax.sharding import PartitionSpec as P

NL = 64
LEVELS = 2 * NL
K = 4
RX = 2
RY = 4
PITCH = 32
MESH = pl.DeviceIdType.MESH
F32 = jnp.float32
BF16 = jnp.bfloat16

time_step = 0.5


def kernel(
    size_x,
    size_y,
    spectrum_h,
    courant_h,
    source_h,
    land_h,
    stokes_h,
    velocity_h,
    coriolis_h,
    ocodes_h,
    oweights_h,
    wcodes_h,
    wweights_h,
    spectrum_o,
    velocity_o,
    current_o,
    cells,
    courant,
    source,
    land,
    stokes_kernel,
    wide,
    middle,
    coriolis,
    ocodes,
    oweights,
    wcodes,
    wweights,
    load_sem,
    edge_f,
    edge_s,
    edge_r,
    south_north,
    vx_s,
    vx_r,
    vy_s,
    vy_r,
    mx_s,
    mx_r,
    my_s,
    my_r,
    strip,
    prof,
    px_s,
    px_r,
    py_s,
    py_r,
    pd_s,
    pd_r,
    select,
    stokes,
    cor,
    coef,
    means,
    ex_s,
    ex_r,
    ey_s,
    ey_r,
    ed_r,
    send_sem,
    recv_sem,
):
    wx, wy, bins = spectrum_o.shape
    ox, oy = velocity_o.shape[:2]
    ix, iy = lax.axis_index("gx"), lax.axis_index("gy")
    at_south, at_north = iy == 0, iy == size_y - 1

    def peer(dx, dy):
        return (lax.rem(ix + dx + size_x, size_x), lax.rem(iy + dy + size_y, size_y))

    straight = ((-1, 0), (1, 0), (0, -1), (0, 1))
    barrier = pltpu.get_barrier_semaphore()
    for step in straight:
        pl.semaphore_signal(barrier, inc=1, device_id=peer(*step), device_id_type=MESH)

    loads = [
        pltpu.make_async_copy(src, dst, load_sem.at[i])
        for i, (src, dst) in enumerate(
            (
                (spectrum_h, cells.at[pl.ds(1, wx)]),
                (velocity_h, wide.at[pl.ds(2, ox), pl.ds(8, oy)]),
                (ocodes_h, ocodes),
                (oweights_h, oweights),
                (coriolis_h, coriolis),
                (wcodes_h, wcodes),
                (wweights_h, wweights),
                (courant_h, courant),
                (source_h, source),
                (land_h, land),
                (stokes_h, stokes_kernel),
            )
        )
    ]
    for load in loads:
        load.start()

    count = [0]

    def remote(src, dst, step):
        i = count[0]
        count[0] += 1
        return pltpu.make_async_remote_copy(
            src_ref=src,
            dst_ref=dst,
            send_sem=send_sem.at[i],
            recv_sem=recv_sem.at[i],
            device_id=peer(*step),
            device_id_type=MESH,
        )

    lane = lax.broadcasted_iota(jnp.int32, (1, LEVELS), 1)
    low = lane < NL

    def swap(value):
        return pltpu.roll(value, NL, 1)

    def pack_x(ref, side, row):
        edge = jnp.where(low, swap(ref[row, pl.ds(8, oy), :]), ref[row + 1, pl.ds(8, oy), :])
        side[...] = edge.astype(BF16)

    def pack_y(ref, side, col):
        edge = jnp.where(low, ref[pl.ds(2, ox), col, :], swap(ref[pl.ds(2, ox), col + 1, :]))
        side[...] = edge.astype(BF16)

    def unpack_x(ref, side, row):
        edge = side[...].astype(F32)
        ref[row, pl.ds(8, oy), :] = swap(edge)
        ref[row + 1, pl.ds(8, oy), :] = edge

    def unpack_y(ref, side, col, outside):
        edge = side[...].astype(F32)
        edge = jnp.where(outside, jnp.zeros_like(edge), edge)
        ref[pl.ds(2, ox), col, :] = edge
        ref[pl.ds(2, ox), col + 1, :] = swap(edge)

    loads[0].wait()
    for x in range(wx):
        row = cells[x + 1].astype(F32)
        for slot, col in enumerate((0, 1, wy - 2, wy - 1)):
            edge_f[slot, x : x + 1, :] = row[col : col + 1]
    edge_s[0] = edge_f[0].astype(BF16)
    edge_s[1] = edge_f[3].astype(BF16)
    loads[1].wait()
    pack_x(wide, vx_s.at[0], 2)
    pack_x(wide, vx_s.at[1], ox)
    pack_y(wide, vy_s.at[0], 8)
    pack_y(wide, vy_s.at[1], 6 + oy)

    pl.semaphore_wait(barrier, 4)
    first = [
        remote(cells.at[wx], cells.at[0], (1, 0)),
        remote(cells.at[1], cells.at[wx + 1], (-1, 0)),
        remote(edge_s.at[1], edge_r.at[0], (0, 1)),
        remote(edge_s.at[0], edge_r.at[1], (0, -1)),
        remote(vx_s.at[1], vx_r.at[0], (1, 0)),
        remote(vx_s.at[0], vx_r.at[1], (-1, 0)),
        remote(vy_s.at[1], vy_r.at[0], (0, 1)),
        remote(vy_s.at[0], vy_r.at[1], (0, -1)),
    ]
    for copy in first[:4]:
        copy.start()

    for load in loads[2:]:
        load.wait()
    prof[...] = jnp.zeros_like(prof)
    means[...] = jnp.zeros_like(means)
    speed_x, speed_y = courant[0:1, :], courant[1:2, :]
    coef[0:1, :] = 1.0 - jnp.abs(speed_x) - jnp.abs(speed_y)
    coef[1:2, :] = jnp.maximum(speed_x, 0.0)
    coef[2:3, :] = jnp.maximum(-speed_x, 0.0)
    coef[3:4, :] = jnp.maximum(speed_y, 0.0)
    coef[4:5, :] = jnp.maximum(-speed_y, 0.0)

    slot_row = lax.broadcasted_iota(jnp.int32, (LEVELS, LEVELS), 0)
    own_cell = lax.rem(lane, oy) // RY

    def choose(i):
        def pair(ref, entry):
            return jnp.concatenate(
                [ref[RX * i, entry : entry + 1, :], ref[RX * i + 1, entry : entry + 1, :]], axis=1
            )

        weights = [pair(oweights, entry) for entry in range(K)]
        total = weights[0] + weights[1] + weights[2] + weights[3]
        rows = jnp.zeros((LEVELS, LEVELS), F32)
        for entry in range(K):
            code = pair(ocodes, entry)
            third = lax.shift_right_logical(code * 11, 5)
            slot = third * (PITCH - 3) + code + own_cell
            rows = rows + jnp.where(slot_row == slot, weights[entry] / total, 0.0)
        rows = rows.T
        high = rows.astype(BF16)
        select[i, :, 0:LEVELS] = high
        select[i, :, LEVELS : 2 * LEVELS] = (rows - high.astype(F32)).astype(BF16)

    @pl.loop(0, wx // 4)
    def _(group):
        for part in range(4):
            choose(4 * group + part)

    growth = land[...].astype(F32)
    gain_rows = growth * (1.0 + 0.2 * source[...])
    damp_rows = 0.1 * growth
    gain, damp = gain_rows.T, damp_rows.T
    for copy in first[:4]:
        copy.wait()
    for side, outside in ((0, at_south), (1, at_north)):
        value = edge_r[side].astype(F32)
        south_north[side] = jnp.where(outside, jnp.zeros_like(value), value)

    chunk = 3 * LEVELS
    cell_x = lax.broadcasted_iota(jnp.int32, (wx, chunk), 0)
    cell_y = lax.broadcasted_iota(jnp.int32, (wy, chunk), 0)

    def updated(span, center, west, east, south, north, gain_x, damp_x):
        advected = (
            coef[0:1, span] * center
            + coef[1:2, span] * west
            + coef[2:3, span] * east
            + coef[3:4, span] * south
            + coef[4:5, span] * north
        )
        return (advected * (gain_x - damp_x * advected)).astype(BF16)

    def update_row(x):
        here = lax.broadcasted_iota(jnp.int32, (wy, wx), 1) == x
        gain_x = jnp.sum(jnp.where(here, gain, 0.0), axis=1, keepdims=True)
        damp_x = jnp.sum(jnp.where(here, damp, 0.0), axis=1, keepdims=True)
        for start in range(0, bins, chunk):
            span = pl.ds(start, chunk)
            center = cells[x + 1, :, span].astype(F32)
            south = jnp.where(cell_y == 0, south_north[0, pl.ds(x, 1), span], pltpu.roll(center, 1, 0))
            north = jnp.where(
                cell_y == wy - 1, south_north[1, pl.ds(x, 1), span], pltpu.roll(center, wy - 1, 0)
            )
            west, east = cells[x, :, span].astype(F32), cells[x + 2, :, span].astype(F32)
            spectrum_o[x, :, span] = updated(span, center, west, east, south, north, gain_x, damp_x)

    def as_profile(value):
        value = jnp.dot(value, stokes_kernel[...], preferred_element_type=F32)
        value = value.astype(BF16).astype(F32)
        return jnp.where(low, swap(value), -swap(value))

    update_row(0)
    update_row(wx - 1)
    strip[0:wx] = spectrum_o[0]
    strip[wx : 2 * wx] = spectrum_o[wx - 1]
    second = [
        remote(px_s.at[1], px_r.at[0], (1, 0)),
        remote(px_s.at[0], px_r.at[1], (-1, 0)),
        remote(py_s.at[1], py_r.at[0], (0, 1)),
        remote(py_s.at[0], py_r.at[1], (0, -1)),
        remote(px_s.at[1], pd_r.at[0], (1, 1)),
        remote(px_s.at[1], pd_r.at[1], (1, -1)),
        remote(px_s.at[0], pd_r.at[2], (-1, 1)),
        remote(px_s.at[0], pd_r.at[3], (-1, -1)),
    ]
    outermost = as_profile(strip[0 : 2 * wx]).astype(BF16)
    px_s[0] = outermost[0:wx]
    px_s[1] = outermost[wx : 2 * wx]
    for copy in second[4:] + second[:2]:
        copy.start()
    for side, col in ((0, 0), (1, wy - 1)):
        for start in range(0, bins, chunk):
            span = pl.ds(start, chunk)
            center = edge_f[3 * side, :, span]
            before = cells[0, :, span].astype(F32)[col : col + 1]
            after = cells[wx + 1, :, span].astype(F32)[col : col + 1]
            west = jnp.where(cell_x == 0, before, pltpu.roll(center, 1, 0))
            east = jnp.where(cell_x == wx - 1, after, pltpu.roll(center, wx - 1, 0))
            inner, outer = edge_f[1 + side, :, span], south_north[side, :, span]
            south, north = (inner, outer) if side else (outer, inner)
            strip[(2 + side) * wx : (3 + side) * wx, span] = updated(
                span, center, west, east, south, north,
                gain_rows[:, col : col + 1], damp_rows[:, col : col + 1],
            )
    outermost = as_profile(strip[2 * wx : 4 * wx]).astype(BF16)
    py_s[0] = outermost[0:wx]
    py_s[1] = outermost[wx : 2 * wx]
    for copy in second[2:4] + first[4:]:
        copy.start()

    @pl.loop(0, wx // 2 - 1)
    def _(group):
        for part in range(2):
            update_row(2 * group + part + 1)

    turned = coriolis[...].T

    @pl.loop(0, ox // 8)
    def _(group):
        for part in range(8):
            x = 8 * group + part
            here = lax.broadcasted_iota(jnp.int32, (oy, ox), 1) == x
            column = jnp.sum(jnp.where(here, turned, 0.0), axis=1, keepdims=True)
            cor[x] = jnp.broadcast_to(column, (oy, LEVELS))

    own = as_profile(spectrum_o[...].reshape(wx * wy, bins))
    prof[pl.ds(1, wx), pl.ds(1, wy), :] = own.reshape(wx, wy, LEVELS)
    for copy in first[4:]:
        copy.wait()
    unpack_x(wide, vx_r.at[0], 0)
    unpack_x(wide, vx_r.at[1], ox + 2)
    unpack_y(wide, vy_r.at[0], 6, at_south)
    unpack_y(wide, vy_r.at[1], 8 + oy, at_north)
    for copy in second:
        copy.wait()
    prof[0, pl.ds(1, wy), :] = px_r[0].astype(F32)
    prof[wx + 1, pl.ds(1, wy), :] = px_r[1].astype(F32)
    for side, outside, col in ((0, at_south, 0), (1, at_north, wy + 1)):
        value = py_r[side].astype(F32)
        prof[pl.ds(1, wx), col, :] = jnp.where(outside, jnp.zeros_like(value), value)
    for i, row, col, outside, line in (
        (0, 0, 0, at_south, wy - 1),
        (1, 0, wy + 1, at_north, 0),
        (2, wx + 1, 0, at_south, wy - 1),
        (3, wx + 1, wy + 1, at_north, 0),
    ):
        value = pd_r[i].astype(F32)[line : line + 1]
        prof[row, col : col + 1, :] = jnp.where(outside, jnp.zeros_like(value), value)

    c1 = jnp.where(low, -8.0 / 12.0, 8.0 / 12.0)
    c2 = jnp.where(low, -1.0 / 12.0, 1.0 / 12.0)

    def block(ref, x, rows, y, cols):
        return ref[pl.ds(x + 2, rows), pl.ds(y + 8, cols), :]

    def absolute(ref, x, rows, y, cols):
        def ahead(step):
            return jnp.where(
                low, block(ref, x, rows, y + step, cols), block(ref, x + step, rows, y, cols)
            )

        turn = c1 * (ahead(1) - ahead(-1)) - c2 * (ahead(2) - ahead(-2))
        return cor[pl.ds(x, rows), pl.ds(y, cols), :] + turn + pltpu.roll(turn, NL, 2)

    def advance(x, rows, y, cols):
        drift = stokes[pl.ds(x, rows), pl.ds(y, cols), :]
        middle[pl.ds(x + 2, rows), pl.ds(y + 8, cols), :] = (
            block(wide, x, rows, y, cols) + time_step * absolute(wide, x, rows, y, cols) * drift
        )

    def drift_row(i):
        near = prof[pl.ds(i, 4)].reshape(4 * PITCH, LEVELS).astype(BF16)
        near = jnp.concatenate([near, near], axis=0)
        both = jnp.dot(select[i], near, preferred_element_type=F32)
        stokes[pl.ds(RX * i, RX)] = both.reshape(RX, oy, LEVELS)

    drift_row(0)
    drift_row(wx - 1)
    advance(0, 2, 0, oy)
    advance(ox - 2, 2, 0, oy)
    pack_x(middle, mx_s.at[0], 2)
    pack_x(middle, mx_s.at[1], ox)
    third = [
        remote(mx_s.at[1], mx_r.at[0], (1, 0)),
        remote(mx_s.at[0], mx_r.at[1], (-1, 0)),
        remote(my_s.at[1], my_r.at[0], (0, 1)),
        remote(my_s.at[0], my_r.at[1], (0, -1)),
    ]
    for copy in third[:2]:
        copy.start()

    for i in range(1, wx - 1):
        drift_row(i)
    for i in range(0, ox, 8):
        advance(i, 8, 0, 8)
        advance(i, 8, oy - 8, 8)

    pack_y(middle, my_s.at[0], 8)
    pack_y(middle, my_s.at[1], 6 + oy)
    for copy in third[2:]:
        copy.start()

    @pl.loop(0, wx)
    def _(i):
        advance(RX * i, RX, 8, oy - 16)

    def finish(x, rows, y, cols):
        rate = absolute(middle, x, rows, y, cols) * stokes[pl.ds(x, rows), pl.ds(y, cols), :]
        old = block(wide, x, rows, y, cols) + block(middle, x, rows, y, cols)
        value = 0.5 * old + (0.5 * time_step) * rate
        velocity_o[pl.ds(x, rows), pl.ds(y, cols), :] = value
        mean_u = jnp.sum(jnp.where(low, value, 0.0), axis=2, keepdims=True)
        mean_v = jnp.sum(jnp.where(low, 0.0, value), axis=2, keepdims=True)
        return mean_u * (1.0 / NL), mean_v * (1.0 / NL)

    def finish_into(table, x, rows, y, cols):
        mean_u, mean_v = finish(x, rows, y, cols)
        for row in range(rows):
            table = jnp.where(lane == x + row, mean_u[row], table)
            table = jnp.where(lane == x + row + NL, mean_v[row], table)
        return table

    inner_cols = lax.fori_loop(
        1,
        wx - 1,
        lambda i, table: finish_into(table, RX * i, RX, 8, oy - 16),
        jnp.zeros((oy - 16, LEVELS), F32),
    )

    target = lax.broadcasted_iota(jnp.int32, (LEVELS, LEVELS), 1)
    origin = lax.broadcasted_iota(jnp.int32, (LEVELS, LEVELS), 0)
    offset = RY * lax.rem(target, wy) + target // wy - 1
    used = lane < (RY + 2) * wy
    spread = jnp.where((origin == (offset & (LEVELS - 1))) & used, 1.0, 0.0)
    repeat = LEVELS // wy
    wave_sum = wweights[:, 0, :] + wweights[:, 1, :] + wweights[:, 2, :] + wweights[:, 3, :]
    tiled = [
        (
            jnp.concatenate([wcodes[:, entry, :]] * repeat, axis=1),
            jnp.concatenate([wweights[:, entry, :] / wave_sum] * repeat, axis=1),
        )
        for entry in range(K)
    ]
    wanted = []
    for a in range(RX + 2):
        number = (RY + 2) * a + lane // wy
        chosen = jnp.zeros((wx, LEVELS), F32)
        for code, weight in tiled:
            chosen = chosen + jnp.where((code == number) & used, weight, 0.0)
        wanted.append(chosen)

    for copy in third:
        copy.wait()
    unpack_x(middle, mx_r.at[0], 0)
    unpack_x(middle, mx_r.at[1], ox + 2)
    unpack_y(middle, my_r.at[0], 6, at_south)
    unpack_y(middle, my_r.at[1], 8 + oy, at_north)

    first_cols = last_cols = jnp.zeros((8, LEVELS), F32)
    for i in range(0, ox, 8):
        first_cols = finish_into(first_cols, i, 8, 0, 8)
        last_cols = finish_into(last_cols, i, 8, oy - 8, 8)
    ey_s[0] = first_cols
    ey_s[1] = last_cols
    fourth = [
        remote(ex_s.at[1], ex_r.at[0], (1, 0)),
        remote(ex_s.at[0], ex_r.at[1], (-1, 0)),
        remote(ey_s.at[1], ey_r.at[0], (0, 1)),
        remote(ey_s.at[0], ey_r.at[1], (0, -1)),
        remote(ey_s.at[1], ed_r.at[0], (1, 1)),
        remote(ey_s.at[0], ed_r.at[1], (1, -1)),
        remote(ey_s.at[1], ed_r.at[2], (-1, 1)),
        remote(ey_s.at[0], ed_r.at[3], (-1, -1)),
    ]
    for copy in fourth[4:] + fourth[2:4]:
        copy.start()
    ends = jnp.zeros((oy, LEVELS), F32)
    for side, x in ((0, 0), (1, ox - 1)):
        mean_u, mean_v = finish(x, 1, 0, oy)
        ends = jnp.where(lane == 2 * side, mean_u[0], ends)
        ends = jnp.where(lane == 2 * side + 1, mean_v[0], ends)
    ends = jnp.concatenate([ends, jnp.zeros((LEVELS - oy, LEVELS), F32)], axis=0).T
    ex_s[0, 0:2, :] = ends[0:2]
    ex_s[1, 0:2, :] = ends[2:4]

    for copy in fourth[:2]:
        copy.start()

    inner_cols = finish_into(inner_cols, 0, RX, 8, oy - 16)
    inner_cols = finish_into(inner_cols, ox - RX, RX, 8, oy - 16)
    blank = jnp.zeros((LEVELS - oy, LEVELS), F32)
    by_row = jnp.concatenate([first_cols, inner_cols, last_cols, blank], axis=0).T
    for c in range(2):
        means[c, pl.ds(8, ox), :] = by_row[c * NL : c * NL + ox]

    for copy in fourth:
        copy.wait()
    for c in range(2):
        means[c, 7:8, :] = ex_r[0, c : c + 1, :]
        means[c, 8 + ox : 9 + ox, :] = ex_r[1, c : c + 1, :]
    for side, line, outside, spot, near in (
        (0, 7, at_south, LEVELS - 1, (0, 2)),
        (1, 0, at_north, oy, (1, 3)),
    ):
        here = lane == spot
        column = ey_r[side].T[:, line : line + 1]
        for c in range(2):
            inner = column[c * NL : c * NL + ox]
            inner = jnp.where(outside, jnp.zeros_like(inner), inner)
            means[c, pl.ds(8, ox), :] = jnp.where(here, inner, means[c, pl.ds(8, ox), :])
            for index, row, source_x in ((near[0], 7, ox - 1), (near[1], 8 + ox, 0)):
                spot_x = c * NL + source_x
                corner = ed_r[index, line : line + 1, spot_x : spot_x + 1]
                corner = jnp.where(outside, jnp.zeros_like(corner), corner)
                means[c, row : row + 1, :] = jnp.where(here, corner, means[c, row : row + 1, :])

    gathered = jnp.concatenate(
        [means[c, pl.ds(7 + a, wx, stride=RX), :] for a in range(RX + 2) for c in range(2)], axis=0
    )
    gathered = jnp.dot(
        gathered, spread, preferred_element_type=F32, precision=lax.Precision.HIGHEST
    )
    for c in range(2):
        total = jnp.zeros((wx, LEVELS), F32)
        for a in range(RX + 2):
            start = (2 * a + c) * wx
            total = total + gathered[start : start + wx] * wanted[a]
        shift = LEVELS // 2
        while shift >= wy:
            total = total + pltpu.roll(total, shift, 1)
            shift //= 2
        current_o[c] = total[:, :wy]


def store(*refs):
    sources, targets, sems = refs[:3], refs[3:6], refs[6]
    copies = [
        pltpu.make_async_copy(source, target, sems.at[i])
        for i, (source, target) in enumerate(zip(sources, targets))
    ]
    for copy in copies:
        copy.start()
    for copy in copies:
        copy.wait()


def solution(mesh):
    size_x, size_y = mesh.shape["gx"], mesh.shape["gy"]

    def step(
        spectrum,
        courant,
        source,
        wave_land,
        stokes_kernel,
        velocity,
        coriolis,
        ocean_codes,
        ocean_weights,
        wave_codes,
        wave_weights,
    ):
        wx, wy, bins = spectrum.shape
        ox, oy, levels = velocity.shape
        turn = lambda value: jnp.transpose(value, (0, 2, 1))
        operands = (
            spectrum,
            courant,
            source,
            wave_land,
            stokes_kernel,
            velocity,
            coriolis,
            turn(ocean_codes),
            turn(ocean_weights),
            turn(wave_codes),
            turn(wave_weights),
        )
        vmem = pltpu.VMEM
        edge_x = vmem((2, oy, levels), BF16)
        edge_y = vmem((2, ox, levels), BF16)
        prof_edge = vmem((2, wx, levels), BF16)
        tile = vmem((2, 8, levels), F32)
        copies = 28
        scratch = [
            vmem((wx + 2, wy, bins), BF16),
            vmem((2, bins), F32),
            vmem((wx, wy), F32),
            vmem((wx, wy), jnp.int32),
            vmem((bins, levels), BF16),
            vmem((ox + 4, oy + 16, levels), F32),
            vmem((ox + 4, oy + 16, levels), F32),
            vmem((ox, oy), F32),
            vmem((ox, K, oy), jnp.int32),
            vmem((ox, K, oy), F32),
            vmem((wx, K, wy), jnp.int32),
            vmem((wx, K, wy), F32),
            pltpu.SemaphoreType.DMA((11,)),
            vmem((4, wx, bins), F32),
            vmem((2, wx, bins), BF16),
            vmem((2, wx, bins), BF16),
            vmem((2, wx, bins), F32),
            edge_x,
            edge_x,
            edge_y,
            edge_y,
            edge_x,
            edge_x,
            edge_y,
            edge_y,
            vmem((4 * wx, bins), BF16),
            vmem((wx + 3, PITCH, levels), F32),
            prof_edge,
            prof_edge,
            prof_edge,
            prof_edge,
            prof_edge,
            vmem((4, wx, levels), BF16),
            vmem((wx, levels, 2 * levels), BF16),
            vmem((ox, oy, levels), F32),
            vmem((ox, oy, levels), F32),
            vmem((8, bins), F32),
            vmem((2, ox + 16, levels), F32),
            tile,
            tile,
            tile,
            tile,
            vmem((4, 8, levels), F32),
            pltpu.SemaphoreType.DMA((copies,)),
            pltpu.SemaphoreType.DMA((copies,)),
        ]
        body = lambda *refs: kernel(size_x, size_y, *refs)
        results = pl.pallas_call(
            body,
            out_shape=(
                pltpu.VMEM((wx, wy, bins), BF16),
                pltpu.VMEM((ox, oy, levels), F32),
                pltpu.VMEM((2, wx, wy), F32),
            ),
            in_specs=[pl.BlockSpec(memory_space=pltpu.HBM)] * len(operands),
            out_specs=(pl.BlockSpec(memory_space=pltpu.VMEM),) * 3,
            scratch_shapes=scratch,
            compiler_params=pltpu.CompilerParams(
                collective_id=0, has_side_effects=True, vmem_limit_bytes=40000000
            ),
            name="coupled_step",
        )(*[pltpu.with_memory_space_constraint(o, pltpu.HBM) for o in operands])
        return pl.pallas_call(
            store,
            out_shape=tuple(jax.ShapeDtypeStruct(r.shape, r.dtype) for r in results),
            in_specs=[pl.BlockSpec(memory_space=pltpu.VMEM)] * 3,
            out_specs=(pl.BlockSpec(memory_space=pltpu.HBM),) * 3,
            scratch_shapes=[pltpu.SemaphoreType.DMA((3,))],
            compiler_params=pltpu.CompilerParams(vmem_limit_bytes=40000000),
            name="store_results",
        )(*[pltpu.with_memory_space_constraint(r, pltpu.VMEM) for r in results])

    return jax.shard_map(
        step,
        mesh=mesh,
        in_specs=(
            P("gx", "gy", None),
            P(),
            P("gx", "gy"),
            P("gx", "gy"),
            P(),
            P("gx", "gy", None),
            P("gx", "gy"),
            P("gx", "gy", None),
            P("gx", "gy", None),
            P("gx", "gy", None),
            P("gx", "gy", None),
        ),
        out_specs=(P("gx", "gy", None), P("gx", "gy", None), P(None, "gx", "gy")),
        check_vma=False,
    )
```
